32 devices in a mesh: row: 4 (over y, core), dp: 8 (over z, x).
Axes of the slice: x: 2, y: 2, z: 4, core: 2. Of those that a mesh axis runs over, the one named last changes fastest.
Arguments:
- latents: bfloat16 [32, 64, 64, 384], P('dp', 'row'), may hold values from -6 to 6
- buckets: int32 [32], P('dp'), may hold values from 0 to 999
- cotangent: bfloat16 [32, 64, 64, 384], P('dp', 'row'), may hold values from -6 to 6
- time_table: bfloat16 [1000, 768], replicated, may hold values from -5 to 5
- w_modulate: bfloat16 [768, 4608], replicated, may hold values from -0.21875 to 0.21875
- conv_block: bfloat16 [9, 768], replicated, may hold values from -1.1953125 to 1.1953125
- w_qkv: bfloat16 [768, 2304], replicated, may hold values from -0.21875 to 0.21875
- w_proj: bfloat16 [768, 768], replicated, may hold values from -0.875 to 0.875
- w_fc1: bfloat16 [768, 3072], replicated, may hold values from -0.21875 to 0.21875
- conv_ffn: bfloat16 [9, 3072], replicated, may hold values from -1.3984375 to 1.3984375
- w_fc2: bfloat16 [3072, 768], replicated, may hold values from -0.109375 to 0.109375
- w_down: bfloat16 [1536, 768], replicated, may hold values from -0.15625 to 0.15625
- w_up: bfloat16 [768, 1536], replicated, may hold values from -0.21875 to 0.21875
Outputs:
- section_output: bfloat16 [32, 64, 64, 384], P('dp', 'row')
- latents_grad: float32 [32, 64, 64, 384], P('dp', 'row')
- time_table_grad: float32 [1000, 768], P(None, 'dp')
- w_modulate_grad: float32 [768, 4608], P('dp')
- conv_block_grad: float32 [9, 768], P(None, 'dp')
- w_qkv_grad: float32 [768, 2304], P('dp')
- w_proj_grad: float32 [768, 768], P('dp')
- w_fc1_grad: float32 [768, 3072], P('dp')
- conv_ffn_grad: float32 [9, 3072], P(None, 'dp')
- w_fc2_grad: float32 [3072, 768], P('dp')
- w_down_grad: float32 [1536, 768], P('dp')
- w_up_grad: float32 [768, 1536], P('dp')
The draws below stay inside these ranges and needn't reach their ends.
All inputs are finite; a program needn't handle non-finite values.
Results may differ from the reference program's by a relative error of at most 0.019.
Values may be sent and summed in bfloat16 or wider, within the bound.
No kernel may reach another device: no remote copies, remote signals or barrier semaphores. Data moves between devices by JAX's collectives and lax.ppermute only.
A program may use at most 384 MiB of HBM per device.

```python
import math
import jax
import jax.numpy as jnp
import numpy as np
from jax import lax

C1 = 384
D = 768
HEADS = 12
FF = 3072
NB = 1000
SIDE = 64
ITEMS = 32


def with_ends(result, rng, least, largest):
    dims = result.shape
    spot = [jax.random.randint(jax.random.fold_in(rng, axis), (), 0, dims[axis]) for axis in range(len(dims))]
    result = result.at[tuple(spot)].set(least)
    longest = dims.index(max(dims))
    spot[longest] = (spot[longest] + 1) % dims[longest]
    return result.at[tuple(spot)].set(largest)


def levels(own_key, shape, split, low, largest):
    loudness, own = 1.0, jax.random.fold_in(own_key, 6)
    for axis_at, shards_of in split:
        steps = jnp.exp(jax.random.uniform(jax.random.fold_in(own, axis_at), (shards_of,), jnp.float32, low / len(split), largest / len(split)))
        loudness = loudness * jnp.repeat(steps, shape[axis_at] // shards_of).reshape([-1 if axis == axis_at else 1 for axis in range(len(shape))])
    return loudness


def cumulative_ranks(amount, skew):
    weights = [(1 << 20) // math.isqrt(rank ** skew) + 1 for rank in range(1, amount + 1)]
    deviation = 1 + sum(weights) // (1 << 30)
    return np.cumsum(np.array([max(1, weight // deviation) for weight in weights]))


def skewed_ids(rng, extent, number_of, lean):
    listing = cumulative_ranks(number_of, lean)
    pick = jax.random.randint(jax.random.fold_in(rng, 1), extent, 0, int(listing[number_of - 1]))
    grade = jnp.searchsorted(jnp.asarray(listing, jnp.int32), pick, side="right")
    return jax.random.permutation(jax.random.fold_in(rng, 2), number_of)[grade].astype(jnp.int32)


def noise(own_key, shape, width, most, cuts=(), dtype=jnp.bfloat16):
    drawn = width * jax.random.normal(own_key, shape, jnp.float32)
    if cuts:
        drawn = drawn * levels(own_key, shape, cuts, -0.22, 0.18)
    return jnp.clip(drawn, -most, most).astype(dtype)


def setup_inputs(seed: int = 0) -> dict:
    splits = jax.random.split(jax.random.key(seed), 14)
    latents = noise(splits[0], (ITEMS, SIDE, SIDE, C1), 1.0, 6.0, ((0, 8), (1, 4)))
    buckets = with_ends(skewed_ids(splits[1], (ITEMS,), NB, 2), jax.random.fold_in(splits[1], 3), 0, NB - 1).astype(jnp.int32)
    cotangent = noise(splits[2], (ITEMS, SIDE, SIDE, C1), 1.0, 6.0, ((0, 8), (1, 4)))
    time_table = noise(splits[3], (NB, D), 1.0, 5.0)
    w_modulate = noise(splits[4], (D, 6 * D), D ** -0.5, 0.21875)
    conv_block = noise(splits[5], (9, D), 0.3, 1.1953125)
    w_qkv = noise(splits[6], (D, 3 * D), D ** -0.5, 0.21875)
    w_proj = noise(splits[7], (D, D), (D // 16) ** -0.5, 0.875)
    w_fc1 = noise(splits[8], (D, FF), D ** -0.5, 0.21875)
    conv_ffn = noise(splits[9], (9, FF), 0.35, 1.3984375)
    w_fc2 = noise(splits[10], (FF, D), FF ** -0.5, 0.109375)
    w_down = noise(splits[11], (4 * C1, D), (4 * C1) ** -0.5, 0.15625)
    w_up = noise(splits[12], (D, 4 * C1), D ** -0.5, 0.21875)
    return dict(latents=latents, buckets=buckets, cotangent=cotangent, time_table=time_table, w_modulate=w_modulate, conv_block=conv_block, w_qkv=w_qkv, w_proj=w_proj, w_fc1=w_fc1, conv_ffn=conv_ffn, w_fc2=w_fc2, w_down=w_down, w_up=w_up)


@jax.custom_vjp
def low(v):
    return lax.optimization_barrier(v.astype(jnp.bfloat16)).astype(jnp.float32)

@jax.custom_vjp
def low_back(v):
    return v

def low_keep(v):
    return (low(v), None)

def low_pass(kept, grad):
    return (grad,)

def back_keep(v):
    return (v, None)

def back_low(kept, grad):
    return (low(grad),)
low.defvjp(low_keep, low_pass)
low_back.defvjp(back_keep, back_low)

def matmul(left_side, right_side):
    return jnp.matmul(left_side, right_side, precision=lax.Precision.HIGHEST)

def normalize(values):
    centered = values - lax.optimization_barrier(jnp.mean(values, axis=-1, keepdims=True))
    return centered * lax.rsqrt(lax.optimization_barrier(jnp.mean(centered * centered, axis=-1, keepdims=True)) + 1e-06)

def depthwise(values_grid, kernel):
    padded = jnp.pad(values_grid, ((0, 0), (1, 1), (1, 1), (0, 0)))
    height_cells, width_cells = (values_grid.shape[1], values_grid.shape[2])
    summed = jnp.zeros_like(values_grid)
    for row_shift in range(3):
        for col_shift in range(3):
            summed = summed + kernel[row_shift * 3 + col_shift] * padded[:, row_shift:row_shift + height_cells, col_shift:col_shift + width_cells]
    return summed

def unshuffle(images):
    number, height_cells, width_cells, channels = images.shape
    pieces = images.reshape(number, height_cells // 2, 2, width_cells // 2, 2, channels)
    pieces = jnp.transpose(pieces, (0, 1, 3, 2, 4, 5))
    return pieces.reshape(number, height_cells // 2, width_cells // 2, 4 * channels)

def reshuffle(patches):
    number, height_cells, width_cells, channels = patches.shape
    pieces = patches.reshape(number, height_cells, width_cells, 2, 2, channels // 4)
    pieces = jnp.transpose(pieces, (0, 1, 3, 2, 4, 5))
    return pieces.reshape(number, 2 * height_cells, 2 * width_cells, channels // 4)

def to_groups(grid):
    number, side_cells, channels = (grid.shape[0], grid.shape[1], grid.shape[3])
    half_side = side_cells // 2
    pieces = grid.reshape(number, half_side, 2, half_side, 2, channels)
    pieces = jnp.transpose(pieces, (0, 2, 4, 1, 3, 5))
    return pieces.reshape(number * 4, half_side * half_side, channels)

def from_groups(groups, number, side_cells):
    half_side = side_cells // 2
    channels = groups.shape[-1]
    pieces = groups.reshape(number, 2, 2, half_side, half_side, channels)
    pieces = jnp.transpose(pieces, (0, 3, 1, 4, 2, 5))
    return pieces.reshape(number, side_cells, side_cells, channels)

def attend(queries, key_rows, value_rows):
    factor = queries.shape[-1] ** (-0.5)
    scores = low_back(matmul(queries, jnp.swapaxes(key_rows, 1, 2))) * factor
    weights_soft = low(jax.nn.softmax(scores, axis=-1))
    return low(low_back(matmul(weights_soft, value_rows)))

def block_forward(latent, embedding, weights):
    w_modulate, conv_block, w_qkv, w_proj, w_fc1, conv_ffn, w_fc2 = weights
    number, side_cells, channels = (latent.shape[0], latent.shape[1], latent.shape[3])
    head_dim = channels // HEADS
    modulation = low_back(matmul(low(jax.nn.silu(embedding)), w_modulate))
    pieces = modulation.reshape(number, 6, 1, 1, channels)
    mixed = latent + depthwise(latent, conv_block)
    normed = low(normalize(mixed) * (1.0 + pieces[:, 1]) + pieces[:, 0])
    groups = to_groups(normed)
    group_cells = groups.shape[1]
    merged_rows = low(low_back(matmul(groups.reshape(-1, channels), w_qkv)))
    heads_view = merged_rows.reshape(number * 4, group_cells, 3, HEADS, head_dim)
    heads_view = jnp.transpose(heads_view, (2, 0, 3, 1, 4)).reshape(3, number * 4 * HEADS, group_cells, head_dim)
    attended = jax.checkpoint(attend)(heads_view[0], heads_view[1], heads_view[2])
    attended = jnp.transpose(attended.reshape(number * 4, HEADS, group_cells, head_dim), (0, 2, 1, 3)).reshape(-1, channels)
    projected = low_back(matmul(attended, w_proj)).reshape(number * 4, group_cells, channels)
    mixed = mixed + pieces[:, 2] * from_groups(projected, number, side_cells)
    normed = low(normalize(mixed) * (1.0 + pieces[:, 4]) + pieces[:, 3])
    hidden = low_back(matmul(normed.reshape(-1, channels), w_fc1)).reshape(number, side_cells, side_cells, -1)
    activated = low(jax.nn.gelu(depthwise(hidden, conv_ffn)))
    output = low_back(matmul(activated.reshape(-1, activated.shape[-1]), w_fc2))
    return mixed + pieces[:, 5] * output.reshape(latent.shape)

def reference(latents, buckets, cotangent, time_table, w_modulate, conv_block, w_qkv, w_proj, w_fc1, conv_ffn, w_fc2, w_down, w_up):
    inputs = tuple((argument.astype(jnp.float32) for argument in (latents, time_table, w_modulate, conv_block, w_qkv, w_proj, w_fc1, conv_ffn, w_fc2, w_down, w_up)))

    def forward(image_field, table_float, w_modulate, conv_block, w_qkv, w_proj, w_fc1, conv_ffn, w_fc2, w_down, w_up):
        weights = (w_modulate, conv_block, w_qkv, w_proj, w_fc1, conv_ffn, w_fc2)
        patches = unshuffle(image_field)
        entering = low(low_back(matmul(patches, w_down)))
        embedding = table_float[buckets]

        def one_item(paired):
            return block_forward(paired[0][None], paired[1][None], weights)[0]
        leaving = lax.map(jax.checkpoint(one_item), (entering, embedding))
        rounded = low(low_back(leaving))
        upsampled = low_back(matmul(rounded, w_up))
        return image_field + reshuffle(upsampled)
    output, pullback = jax.vjp(forward, *inputs)
    gradients = pullback(cotangent.astype(jnp.float32))
    return (output.astype(jnp.bfloat16), gradients[0], gradients[1], gradients[2], gradients[3], gradients[4], gradients[5], gradients[6], gradients[7], gradients[8], gradients[9], gradients[10])
```

```python
from functools import partial

import jax
import jax.numpy as jnp
from jax import lax
from jax.sharding import PartitionSpec as P

HEADS = 12


def rounders():

    @jax.custom_vjp
    def low(value):
        return lax.optimization_barrier(value.astype(jnp.bfloat16)).astype(jnp.float32)

    def low_keep(value):
        return (low(value), None)

    def low_pass(kept, grad):
        return (grad,)

    low.defvjp(low_keep, low_pass)

    @jax.custom_vjp
    def low_back(value):
        return value

    def back_keep(value):
        return (value, None)

    def back_low(kept, grad):
        return (low(grad),)

    low_back.defvjp(back_keep, back_low)

    @jax.custom_vjp
    def product(left_side, right_side):
        return jnp.matmul(
            left_side.astype(jnp.bfloat16),
            right_side.astype(jnp.bfloat16),
            preferred_element_type=jnp.float32,
        )

    def product_keep(left_side, right_side):
        left_half = left_side.astype(jnp.bfloat16)
        right_half = right_side.astype(jnp.bfloat16)
        return (
            jnp.matmul(left_half, right_half, preferred_element_type=jnp.float32),
            (left_half, right_half),
        )

    def product_back(saved_pair, gradient):
        left_half, right_half = saved_pair
        gradient_half = gradient.astype(jnp.bfloat16)
        left_grad = jnp.matmul(
            gradient_half, jnp.swapaxes(right_half, -1, -2), preferred_element_type=jnp.float32
        )
        right_grad = jnp.matmul(
            jnp.swapaxes(left_half, -1, -2), gradient_half, preferred_element_type=jnp.float32
        )
        return (left_grad, right_grad)

    product.defvjp(product_keep, product_back)
    return (low, low_back, product)


def normalize(values):
    centered = values - jnp.mean(values, axis=-1, keepdims=True)
    return centered * lax.rsqrt(jnp.mean(centered * centered, axis=-1, keepdims=True) + 1e-06)


def depthwise(values_grid, kernel):
    padded = jnp.pad(values_grid, ((0, 0), (1, 1), (1, 1), (0, 0)))
    height_cells, width_cells = (values_grid.shape[1], values_grid.shape[2])
    summed = jnp.zeros_like(values_grid)
    for row_shift in range(3):
        for col_shift in range(3):
            summed = (
                summed
                + kernel[row_shift * 3 + col_shift]
                * padded[
                    :, row_shift : row_shift + height_cells, col_shift : col_shift + width_cells
                ]
            )
    return summed


def unshuffle(images):
    number, height_cells, width_cells, channels = images.shape
    pieces = images.reshape(number, height_cells // 2, 2, width_cells // 2, 2, channels)
    pieces = jnp.transpose(pieces, (0, 1, 3, 2, 4, 5))
    return pieces.reshape(number, height_cells // 2, width_cells // 2, 4 * channels)


def reshuffle(patches):
    number, height_cells, width_cells, channels = patches.shape
    pieces = patches.reshape(number, height_cells, width_cells, 2, 2, channels // 4)
    pieces = jnp.transpose(pieces, (0, 1, 3, 2, 4, 5))
    return pieces.reshape(number, 2 * height_cells, 2 * width_cells, channels // 4)


def to_groups(grid):
    number, side_cells, channels = (grid.shape[0], grid.shape[1], grid.shape[3])
    half_side = side_cells // 2
    pieces = grid.reshape(number, half_side, 2, half_side, 2, channels)
    pieces = jnp.transpose(pieces, (0, 2, 4, 1, 3, 5))
    return pieces.reshape(number * 4, half_side * half_side, channels)


def from_groups(groups, number, side_cells):
    half_side = side_cells // 2
    channels = groups.shape[-1]
    pieces = groups.reshape(number, 2, 2, half_side, half_side, channels)
    pieces = jnp.transpose(pieces, (0, 3, 1, 4, 2, 5))
    return pieces.reshape(number, side_cells, side_cells, channels)


def attend(queries, key_rows, value_rows, helpers):
    low, low_back, product = helpers
    factor = queries.shape[-1] ** (-0.5)
    scores = low_back(product(queries, jnp.swapaxes(key_rows, 1, 2))) * factor
    weights_soft = low(jax.nn.softmax(scores, axis=-1))
    return low(low_back(product(weights_soft, value_rows)))


def block_forward(latent, modulation, weights, helpers):
    low, low_back, product = helpers
    conv_block, w_qkv, w_proj, w_fc1, conv_ffn, w_fc2 = weights
    number, side_cells, channels = (latent.shape[0], latent.shape[1], latent.shape[3])
    head_dim = channels // HEADS
    pieces = low_back(modulation).reshape(number, 6, 1, 1, channels)
    mixed = latent + depthwise(latent, conv_block)
    normed = low(normalize(mixed) * (1.0 + pieces[:, 1]) + pieces[:, 0])
    groups = to_groups(normed)
    group_cells = groups.shape[1]
    merged_rows = low(low_back(product(groups.reshape(-1, channels), w_qkv)))
    heads_view = merged_rows.reshape(number * 4, group_cells, 3, HEADS, head_dim)
    heads_view = jnp.transpose(heads_view, (2, 0, 3, 1, 4)).reshape(
        3, number * 4 * HEADS, group_cells, head_dim
    )
    attended = jax.checkpoint(partial(attend, helpers=helpers))(
        heads_view[0], heads_view[1], heads_view[2]
    )
    attended = jnp.transpose(
        attended.reshape(number * 4, HEADS, group_cells, head_dim), (0, 2, 1, 3)
    ).reshape(-1, channels)
    projected = low_back(product(attended, w_proj)).reshape(number * 4, group_cells, channels)
    mixed = mixed + pieces[:, 2] * from_groups(projected, number, side_cells)
    normed = low(normalize(mixed) * (1.0 + pieces[:, 4]) + pieces[:, 3])
    hidden = low_back(product(normed.reshape(-1, channels), w_fc1)).reshape(
        number, side_cells, side_cells, -1
    )
    activated = low(jax.nn.gelu(depthwise(hidden, conv_ffn)))
    output = low_back(product(activated.reshape(-1, activated.shape[-1]), w_fc2))
    return mixed + pieces[:, 5] * output.reshape(latent.shape)


def own_columns(values, index, count):
    width = values.shape[1] // count
    return lax.dynamic_slice_in_dim(values, index * width, width, axis=1)


def modulate_grads(modulation_grad, buckets, time_table, w_modulate):
    dp_count = lax.axis_size("dp")
    dp_index = lax.axis_index("dp")
    every_grad = lax.all_gather(modulation_grad, ("dp", "row"), axis=0, tiled=True)
    every_bucket = lax.all_gather(buckets, "dp", axis=0, tiled=True)
    own_part = own_columns(time_table[every_bucket], dp_index, dp_count).astype(jnp.float32)
    active = jax.nn.silu(own_part).astype(jnp.bfloat16)
    modulate_grad = jnp.einsum("id,if->df", active, every_grad, preferred_element_type=jnp.float32)
    rows = time_table.shape[1] // dp_count
    own_rows = lax.dynamic_slice_in_dim(w_modulate, dp_index * rows, rows, axis=0)
    active_grad = jnp.einsum("if,df->id", every_grad, own_rows, preferred_element_type=jnp.float32)
    sigmoid = jax.nn.sigmoid(own_part)
    embedding_grad = active_grad * sigmoid * (1.0 + own_part * (1.0 - sigmoid))
    selector = (
        lax.iota(jnp.int32, time_table.shape[0])[:, None] == every_bucket[None, :]
    ).astype(jnp.float32)
    table_grad = jnp.matmul(selector, embedding_grad, precision=lax.Precision.HIGHEST)
    return (table_grad, modulate_grad)


def bit_count(size):
    return size.bit_length() - 1


def swap(value, axis_name, bit):
    size = lax.axis_size(axis_name)
    return lax.ppermute(value, axis_name, [(k, k ^ (1 << bit)) for k in range(size)])


def own_bit(axis_name, bit):
    return (lax.axis_index(axis_name) >> bit) & 1


def added(kept, received):
    return (kept.astype(jnp.float32) + received.astype(jnp.float32)).astype(jnp.bfloat16)


def pick(value, index, axis):
    return lax.dynamic_index_in_dim(value, index, axis=axis, keepdims=False)


LANES = 384


def reduce_group(arrays):
    dp_count, row_count = (lax.axis_size("dp"), lax.axis_size("row"))
    core = own_bit("row", 0)
    blocks = []
    for array in arrays:
        columns = array.shape[1] // 2
        kept = lax.dynamic_slice_in_dim(array, core * columns, columns, axis=1)
        sent = lax.dynamic_slice_in_dim(array, (1 - core) * columns, columns, axis=1)
        half = added(kept, swap(sent, "row", 0)).reshape(dp_count, array.shape[0] // dp_count, columns)
        for start in range(0, columns, LANES):
            blocks.append(half[:, :, start : start + LANES])
    joined = jnp.concatenate(blocks, axis=1)
    d_bits = [("dp", bit) for bit in range(bit_count(dp_count))]
    y_bits = [("row", bit) for bit in range(1, bit_count(row_count))]
    orders = [
        y_bits + d_bits,
        d_bits[:2] + y_bits + d_bits[2:],
        d_bits[1:2] + y_bits + d_bits[:1] + d_bits[2:],
    ]
    dims = d_bits[::-1] + y_bits[::-1]
    total = joined.shape[1]
    parts = joined.reshape((2,) * len(dims) + (3, total // 3 // (row_count // 2), LANES))
    values = [pick(parts, k, len(dims)) for k in range(3)]
    left = [list(dims) for _ in range(3)]
    for step in range(len(dims)):
        for k in range(3):
            at = left[k].index(orders[k][step])
            mine = own_bit(*orders[k][step])
            received = swap(pick(values[k], 1 - mine, at), *orders[k][step])
            values[k] = added(pick(values[k], mine, at), received)
            left[k].pop(at)
    result = jnp.stack(values)
    for name, bit in [*y_bits, ("row", 0)]:
        other = swap(result, name, bit)
        mine = own_bit(name, bit)
        result = jnp.stack([jnp.where(mine == 0, result, other), jnp.where(mine == 0, other, result)])
    result = result.reshape(2, total, LANES).astype(jnp.float32)
    outputs, at = ([], 0)
    for array in arrays:
        rows = array.shape[0] // dp_count
        pieces = []
        for side in range(2):
            for k in range(array.shape[1] // 2 // LANES):
                pieces.append(result[side, at + k * rows : at + (k + 1) * rows])
        at += rows * (array.shape[1] // 2 // LANES)
        outputs.append(jnp.concatenate(pieces, axis=1))
    return outputs


def body(
    latents,
    buckets,
    cotangent,
    time_table,
    w_modulate,
    conv_block,
    w_qkv,
    w_proj,
    w_fc1,
    conv_ffn,
    w_fc2,
    w_down,
    w_up,
):
    helpers = rounders()
    row_count = lax.axis_size("row")
    row_index = lax.axis_index("row")
    per_device = latents.shape[0] // row_count
    own_buckets = lax.dynamic_slice_in_dim(buckets, row_index * per_device, per_device)
    block_weights = tuple(
        (weight.astype(jnp.float32) for weight in (conv_block, w_qkv, w_proj, w_fc1, conv_ffn, w_fc2))
    )
    patches = unshuffle(latents)
    cot_patches = unshuffle(cotangent)

    def local_block(entering, modulation, *weights):
        return block_forward(entering, modulation, weights, helpers)

    own_table = time_table[own_buckets].astype(jnp.float32)
    modulation = jnp.matmul(
        jax.nn.silu(own_table).astype(jnp.bfloat16), w_modulate, preferred_element_type=jnp.float32
    )
    sending = jnp.einsum(
        "abce,ed->abcd", patches, w_down, preferred_element_type=jnp.float32
    ).astype(jnp.bfloat16)
    entering_half = lax.all_to_all(sending, "row", split_axis=0, concat_axis=1, tiled=True)
    leaving, pullback = jax.vjp(
        local_block, entering_half.astype(jnp.float32), modulation, *block_weights
    )
    leaving_half = leaving.astype(jnp.bfloat16)
    returned_half = lax.all_to_all(leaving_half, "row", split_axis=1, concat_axis=0, tiled=True)
    upsampled = jnp.einsum("abcd,de->abce", returned_half, w_up, preferred_element_type=jnp.float32)
    output = (latents.astype(jnp.float32) + reshuffle(upsampled)).astype(jnp.bfloat16)
    leaving_grad = jnp.einsum(
        "abce,de->abcd", cot_patches, w_up, preferred_element_type=jnp.float32
    ).astype(jnp.bfloat16)
    up_grad = jnp.einsum(
        "abcd,abce->de", returned_half, cot_patches, preferred_element_type=jnp.float32
    )
    arrived_grad = lax.all_to_all(leaving_grad, "row", split_axis=0, concat_axis=1, tiled=True)
    gradients = pullback(arrived_grad.astype(jnp.float32))
    entering_grad = lax.all_to_all(
        gradients[0].astype(jnp.bfloat16), "row", split_axis=1, concat_axis=0, tiled=True
    )
    down_grad = jnp.einsum(
        "abce,abcd->ed", patches, entering_grad, preferred_element_type=jnp.float32
    )
    patch_back = jnp.einsum(
        "abcd,ed->abce", entering_grad, w_down, preferred_element_type=jnp.float32
    )
    latents_grad = cotangent.astype(jnp.float32) + reshuffle(patch_back)
    table_grad, modulate_grad = modulate_grads(
        gradients[1].astype(jnp.bfloat16), buckets, time_table, w_modulate
    )
    conv_grads = jnp.concatenate([gradients[2], gradients[6]], axis=1)
    conv_all = lax.psum(conv_grads, ("row", "dp"))
    dp_index = lax.axis_index("dp")
    dp_count = lax.axis_size("dp")
    width = gradients[2].shape[1]
    conv_block_grad = own_columns(conv_all[:, :width], dp_index, dp_count)
    conv_ffn_grad = own_columns(conv_all[:, width:], dp_index, dp_count)
    half = jnp.bfloat16
    early = reduce_group([gradients[5].astype(half), gradients[7].astype(half), up_grad.astype(half)])
    late = reduce_group([gradients[3].astype(half), gradients[4].astype(half), down_grad.astype(half)])
    return (
        output,
        latents_grad,
        table_grad,
        modulate_grad,
        conv_block_grad,
        late[0],
        late[1],
        early[0],
        conv_ffn_grad,
        early[1],
        late[2],
        early[2],
    )


def solution(mesh):
    in_specs = (
        P("dp", "row", None, None),
        P("dp"),
        P("dp", "row", None, None),
        P(),
        P(),
        P(),
        P(),
        P(),
        P(),
        P(),
        P(),
        P(),
        P(),
    )
    out_specs = (
        P("dp", "row", None, None),
        P("dp", "row", None, None),
        P(None, "dp"),
        P("dp", None),
        P(None, "dp"),
        P("dp", None),
        P("dp", None),
        P("dp", None),
        P(None, "dp"),
        P("dp", None),
        P("dp", None),
        P("dp", None),
    )
    return jax.shard_map(body, mesh=mesh, in_specs=in_specs, out_specs=out_specs, check_vma=False)
```

```python
import jax
import jax.numpy as jnp
from jax import lax
from jax.experimental import pallas as pl
from jax.experimental.pallas import tpu as pltpu
from jax.sharding import PartitionSpec as P


HEADS = 12
ROW = 16
FF_WIDTH = 256
F32 = jnp.float32
HALF = jnp.bfloat16
NN = (((1,), (0,)), ((), ()))
NT = (((1,), (1,)), ((), ()))
TN = (((0,), (0,)), ((), ()))
VMEM_LIMIT = 60 * 1024 * 1024


def dot(left, right, dims):
    return lax.dot_general(left, right, dims, preferred_element_type=F32)


def params():
    return pltpu.CompilerParams(vmem_limit_bytes=VMEM_LIMIT)


def cost(flops, moved):
    return pl.CostEstimate(flops=int(flops), bytes_accessed=int(moved), transcendentals=0)


def whole(shape):
    zeros = (0,) * len(shape)
    return pl.BlockSpec(shape, lambda *_: zeros)


def shifted(block, odd):
    at = lax.broadcasted_iota(jnp.int32, block.shape, 0)
    if odd:
        return jnp.where(at == 0, 0.0, pltpu.roll(block, 1, 0))
    return jnp.where(at == ROW - 1, 0.0, pltpu.roll(block, ROW - 1, 0))


def clear_edges(plain, moved):
    rows = plain.shape[1]
    zero = jnp.zeros((ROW, plain.shape[2]), plain.dtype)
    for group in range(4):
        for ref in (plain, moved):
            ref[group, pl.ds(0, ROW), :] = zero
            ref[group, pl.ds(rows - ROW, ROW), :] = zero


def place(plain, moved, group, start, lanes, block):
    plain[group, pl.ds(start, ROW), lanes] = block
    moved[group, pl.ds(start, ROW), lanes] = shifted(block, group % 2 == 1)


ROW_SITES = (((1, -1), (0, 0), (1, 0)), ((0, 0), (1, 0), (0, 1)))
COL_SITES = (((1, True), (0, False), (1, False)), ((0, False), (1, False), (0, True)))


def read_sites(plain, moved, start, lanes):
    sites = {}
    for row_group, offset in ((1, -1), (0, 0), (1, 0), (0, 1)):
        for col_group, is_moved in ((0, False), (1, False), (1, True), (0, True)):
            ref = moved if is_moved else plain
            at = pl.multiple_of(start + offset * ROW, ROW)
            sites[row_group, offset, col_group, is_moved] = ref[
                2 * row_group + col_group, pl.ds(at, ROW), lanes
            ]
    return sites


def tap_values(sites, group):
    values = []
    for down in range(3):
        for across in range(3):
            values.append(sites[ROW_SITES[group // 2][down] + COL_SITES[group % 2][across]])
    return values


def convolve(sites, taps, group):
    values = tap_values(sites, group)
    total = values[0] * taps[0]
    for k in range(1, 9):
        total = total + values[k] * taps[k]
    return total


def tap_rows(kernel_ref, lanes, flip):
    return [kernel_ref[pl.ds(8 - k if flip else k, 1), lanes] for k in range(9)]


def normal_parts(values):
    centered = values - jnp.mean(values, axis=-1, keepdims=True)
    scale = lax.rsqrt(jnp.mean(centered * centered, axis=-1, keepdims=True) + 1e-06)
    return centered * scale, scale


def normal_back(grad, unit, scale):
    average = jnp.mean(grad, axis=-1, keepdims=True)
    along = jnp.mean(grad * unit, axis=-1, keepdims=True)
    return scale * (grad - average - unit * along)


def head_masks(rows):
    low_lanes = lax.broadcasted_iota(jnp.int32, (rows, 128), 1) < 64
    first = jnp.where(low_lanes, 1.0, 0.0)
    return first.astype(HALF), (1.0 - first).astype(HALF)


def at_source(row_block, blocks_each):
    return row_block // blocks_each, pl.multiple_of((row_block % blocks_each) * ROW, ROW)


def attention_forward(arrived, pieces, conv_block, w_qkv, w_proj):
    sources, _, part, width = arrived.shape
    cells = sources * part

    def kernel(
        arrived, pieces, taps, w_qkv, w_proj, mixed_one, normed_one, merged, attended, mixed_two, normed_two, plain, moved, mixed
    ):
        step = pl.program_id(0)

        @pl.when(step == 0)
        def _():
            clear_edges(plain, moved)

            def fill(row, carry):
                source, start = at_source(row, part // ROW)
                to = pl.multiple_of((row + 1) * ROW, ROW)
                for group in range(4):
                    block = arrived[source, group, pl.ds(start, ROW), :].astype(F32)
                    place(plain, moved, group, to, slice(None), block)
                return carry

            lax.fori_loop(0, cells // ROW, fill, 0)

            def lane_step(lane, carry):
                lanes = pl.ds(pl.multiple_of(lane * 128, 128), 128)
                rows = tap_rows(taps, lanes, False)

                def conv_step(row, carry):
                    at = pl.multiple_of((row + 1) * ROW, ROW)
                    sites = read_sites(plain, moved, at, lanes)
                    for group in range(4):
                        mixed[group, pl.ds(pl.multiple_of(row * ROW, ROW), ROW), lanes] = sites[
                            (group // 2, 0, group % 2, False)
                        ] + convolve(sites, rows, group)
                    return carry

                return lax.fori_loop(0, cells // ROW, conv_step, carry)

            lax.fori_loop(0, width // 128, lane_step, 0)

        values = mixed[step]
        mixed_one[0] = values
        unit, _ = normal_parts(values)
        normed_one[0] = (unit * (1.0 + pieces[1:2, :]) + pieces[0:1, :]).astype(HALF)
        for k in range(3):
            merged[0, :, k * width : (k + 1) * width] = dot(
                normed_one[0], w_qkv[:, k * width : (k + 1) * width], NN
            ).astype(HALF)
        masks = head_masks(cells)

        def pair(k, carry):
            at = pl.multiple_of(k * 128, 128)
            queries = merged[0, :, pl.ds(at, 128)] * jnp.asarray(0.125, HALF)
            keys = merged[0, :, pl.ds(width + at, 128)]
            values = merged[0, :, pl.ds(2 * width + at, 128)]
            total = None
            for mask in masks:
                scores = dot(queries * mask, keys, NT)
                scores = jnp.exp(scores - jnp.max(scores, axis=-1, keepdims=True))
                share = 1.0 / jnp.sum(scores, axis=-1, keepdims=True)
                result = dot(scores.astype(HALF), values * mask, NN) * share
                total = result if total is None else total + result
            attended[0, :, pl.ds(at, 128)] = total.astype(HALF)
            return carry

        lax.fori_loop(0, HEADS // 2, pair, 0)
        values = mixed[step] + pieces[2:3, :] * dot(attended[0], w_proj[...], NN)
        mixed_two[0] = values
        unit, _ = normal_parts(values)
        normed_two[0] = (unit * (1.0 + pieces[4:5, :]) + pieces[3:4, :]).astype(HALF)

    def group_block(columns):
        return pl.BlockSpec((1, cells, columns), lambda g: (g, 0, 0))

    def array(columns, dtype):
        return jax.ShapeDtypeStruct((4, cells, columns), dtype)

    return pl.pallas_call(
        kernel,
        name="attention_forward",
        grid=(4,),
        in_specs=[whole(v.shape) for v in (arrived, pieces, conv_block, w_qkv, w_proj)],
        out_specs=[group_block(width * k) for k in (1, 1, 3, 1, 1, 1)],
        out_shape=[
            array(width, F32),
            array(width, HALF),
            array(3 * width, HALF),
            array(width, HALF),
            array(width, F32),
            array(width, HALF),
        ],
        scratch_shapes=[
            pltpu.VMEM((4, cells + 2 * ROW, width), F32),
            pltpu.VMEM((4, cells + 2 * ROW, width), F32),
            pltpu.VMEM((4, cells, width), F32),
        ],
        compiler_params=params(),
        cost_estimate=cost(12e9, 25e6),
    )(arrived, pieces, conv_block, w_qkv, w_proj)


def fill_from(plain, moved, group, values):
    cells = values.shape[0]
    plain[group, pl.ds(ROW, cells), :] = values
    at = lax.broadcasted_iota(jnp.int32, values.shape, 0) % ROW
    if group % 2 == 1:
        side = jnp.where(at == 0, 0.0, pltpu.roll(values, 1, 0))
    else:
        side = jnp.where(at == ROW - 1, 0.0, pltpu.roll(values, cells - 1, 0))
    moved[group, pl.ds(ROW, cells), :] = side


ROOT = 0.7978845608028654


def gelu(values):
    return 0.5 * values * (1.0 + jnp.tanh(ROOT * (values + 0.044715 * (values * values * values))))


def gelu_pair(values):
    square = values * values
    bend = jnp.tanh(ROOT * values * (1.0 + 0.044715 * square))
    half = 0.5 * (1.0 + bend)
    slope = half + 0.5 * values * (1.0 - bend * bend) * (ROOT + (3.0 * 0.044715 * ROOT) * square)
    return values * half, slope


def ffn_forward(normed_two, mixed_two, pieces, w_fc1, conv_ffn, w_fc2, sources):
    _, cells, width = normed_two.shape
    hidden_width = w_fc1.shape[1]
    part = cells // sources
    steps = hidden_width // FF_WIDTH

    def kernel(normed, mixed, pieces, w_one, taps, w_two, hidden, product, leaving, plain, moved, active, total):
        step = pl.program_id(0)

        @pl.when(step == 0)
        def _():
            clear_edges(plain, moved)
            total[...] = jnp.zeros_like(total)

        for group in range(4):
            values = dot(normed[group], w_one[...], NN)
            hidden[group] = values.astype(HALF)
            fill_from(plain, moved, group, values)

        for lane in range(FF_WIDTH // 128):
            lanes = slice(lane * 128, (lane + 1) * 128)
            rows = tap_rows(taps, lanes, False)

            def conv_step(row, carry):
                at = pl.multiple_of((row + 1) * ROW, ROW)
                sites = read_sites(plain, moved, at, lanes)
                for group in range(4):
                    to = pl.ds(pl.multiple_of(group * cells + row * ROW, ROW), ROW)
                    active[to, lanes] = gelu(convolve(sites, rows, group)).astype(HALF)
                return carry

            lax.fori_loop(0, cells // ROW, conv_step, 0)
        total[...] += dot(active[...], w_two[...], NN)

        @pl.when(step == steps - 1)
        def _():
            for group in range(4):
                values = total[pl.ds(group * cells, cells), :]
                product[group] = values.astype(HALF)
                values = (mixed[group] + pieces[5:6, :] * values).astype(HALF)
                for source in range(sources):
                    leaving[source, group] = values[source * part : (source + 1) * part]

    return pl.pallas_call(
        kernel,
        name="ffn_forward",
        grid=(steps,),
        in_specs=[
            whole(normed_two.shape),
            whole(mixed_two.shape),
            whole(pieces.shape),
            pl.BlockSpec((width, FF_WIDTH), lambda k: (0, k)),
            pl.BlockSpec((9, FF_WIDTH), lambda k: (0, k)),
            pl.BlockSpec((FF_WIDTH, width), lambda k: (k, 0)),
        ],
        out_specs=[
            pl.BlockSpec((4, cells, FF_WIDTH), lambda k: (0, 0, k)),
            whole((4, cells, width)),
            whole((sources, 4, part, width)),
        ],
        out_shape=[
            jax.ShapeDtypeStruct((4, cells, hidden_width), HALF),
            jax.ShapeDtypeStruct((4, cells, width), HALF),
            jax.ShapeDtypeStruct((sources, 4, part, width), HALF),
        ],
        scratch_shapes=[
            pltpu.VMEM((4, cells + 2 * ROW, FF_WIDTH), F32),
            pltpu.VMEM((4, cells + 2 * ROW, FF_WIDTH), F32),
            pltpu.VMEM((4 * cells, FF_WIDTH), HALF),
            pltpu.VMEM((4 * cells, width), F32),
        ],
        compiler_params=params(),
        cost_estimate=cost(20e9, 25e6),
    )(normed_two, mixed_two, pieces, w_fc1, conv_ffn, w_fc2)


def ffn_backward(arrived, product, normed_two, mixed_two, hidden, pieces, w_fc1, conv_ffn, w_fc2):
    sources, _, part, width = arrived.shape
    cells = sources * part
    hidden_width = w_fc1.shape[1]
    steps = hidden_width // FF_WIDTH

    def kernel(
        arrived, product, normed, mixed, hidden, pieces, w_one, taps, w_two,
        one_grad, two_grad, tap_grad, mixed_grad, vectors,
        plain, moved, grad_plain, grad_moved, active, hidden_grad, gated, total,
    ):
        step = pl.program_id(0)

        @pl.when(step == 0)
        def _():
            clear_edges(plain, moved)
            clear_edges(grad_plain, grad_moved)
            total[...] = jnp.zeros_like(total)
            for group in range(4):
                for source in range(sources):
                    to = pl.ds(group * cells + source * part, part)
                    gated[to, :] = (arrived[source, group].astype(F32) * pieces[5:6, :]).astype(HALF)

        for group in range(4):
            fill_from(plain, moved, group, hidden[group].astype(F32))
            grad_plain[group, pl.ds(ROW, cells), :] = dot(
                gated[pl.ds(group * cells, cells), :], w_two[...], NT
            )

        for lane in range(FF_WIDTH // 128):
            lanes = slice(lane * 128, (lane + 1) * 128)
            rows = tap_rows(taps, lanes, False)
            flipped = tap_rows(taps, lanes, True)

            def gelu_step(row, sums):
                at = pl.multiple_of((row + 1) * ROW, ROW)
                sites = read_sites(plain, moved, at, lanes)
                sums = list(sums)
                for group in range(4):
                    values = tap_values(sites, group)
                    result, slope = gelu_pair(convolve(sites, rows, group))
                    to = pl.ds(pl.multiple_of(group * cells + row * ROW, ROW), ROW)
                    active[to, lanes] = result.astype(HALF)
                    grad = grad_plain[group, pl.ds(at, ROW), lanes] * slope
                    place(grad_plain, grad_moved, group, at, lanes, grad)
                    for k in range(9):
                        both = values[k] * grad
                        sums[k] = sums[k] + (both[:8] + both[8:])
                return tuple(sums)

            start = tuple(jnp.zeros((8, 128), F32) for _ in range(9))
            sums = lax.fori_loop(0, cells // ROW, gelu_step, start)
            for k in range(9):
                tap_grad[k : k + 1, lanes] = jnp.sum(sums[k], axis=0, keepdims=True)

            def back_step(row, carry):
                at = pl.multiple_of((row + 1) * ROW, ROW)
                sites = read_sites(grad_plain, grad_moved, at, lanes)
                for group in range(4):
                    to = pl.ds(pl.multiple_of(group * cells + row * ROW, ROW), ROW)
                    hidden_grad[to, lanes] = convolve(sites, flipped, group).astype(HALF)
                return carry

            lax.fori_loop(0, cells // ROW, back_step, 0)

        two_grad[...] = dot(active[...], gated[...], TN).astype(HALF)
        grads = hidden_grad[...]
        one = None
        for group in range(4):
            term = dot(normed[group], hidden_grad[pl.ds(group * cells, cells), :], TN)
            one = term if one is None else one + term
        one_grad[...] = one.astype(HALF)
        total[...] += dot(grads, w_one[...], NT)

        @pl.when(step == steps - 1)
        def _():
            shift_sum = jnp.zeros((1, width), F32)
            scale_sum = jnp.zeros((1, width), F32)
            gate_sum = jnp.zeros((1, width), F32)
            for group in range(4):
                for source in range(sources):
                    to = pl.ds(source * part, part)
                    unit, scale = normal_parts(mixed[group, to, :])
                    grad = total[pl.ds(group * cells + source * part, part), :]
                    came = arrived[source, group].astype(F32)
                    shift_sum += jnp.sum(grad, axis=0, keepdims=True)
                    scale_sum += jnp.sum(grad * unit, axis=0, keepdims=True)
                    gate_sum += jnp.sum(came * product[group, to, :].astype(F32), axis=0, keepdims=True)
                    mixed_grad[group, to, :] = came + normal_back(
                        grad * (1.0 + pieces[4:5, :]), unit, scale
                    )
            vectors[0:1, :] = shift_sum
            vectors[1:2, :] = scale_sum
            vectors[2:3, :] = gate_sum

    def once(value):
        zeros = (0,) * value.ndim
        return pl.BlockSpec(value.shape, lambda k: zeros, pipeline_mode=pl.Buffered(1))

    return pl.pallas_call(
        kernel,
        name="ffn_backward",
        grid=(steps,),
        in_specs=[
            once(arrived),
            once(product),
            once(normed_two),
            once(mixed_two),
            pl.BlockSpec((4, cells, FF_WIDTH), lambda k: (0, 0, k)),
            once(pieces),
            pl.BlockSpec((width, FF_WIDTH), lambda k: (0, k)),
            pl.BlockSpec((9, FF_WIDTH), lambda k: (0, k)),
            pl.BlockSpec((FF_WIDTH, width), lambda k: (k, 0)),
        ],
        out_specs=[
            pl.BlockSpec((width, FF_WIDTH), lambda k: (0, k)),
            pl.BlockSpec((FF_WIDTH, width), lambda k: (k, 0)),
            pl.BlockSpec((9, FF_WIDTH), lambda k: (0, k)),
            whole((4, cells, width)),
            whole((3, width)),
        ],
        out_shape=[
            jax.ShapeDtypeStruct((width, hidden_width), HALF),
            jax.ShapeDtypeStruct((hidden_width, width), HALF),
            jax.ShapeDtypeStruct((9, hidden_width), F32),
            jax.ShapeDtypeStruct((4, cells, width), F32),
            jax.ShapeDtypeStruct((3, width), F32),
        ],
        scratch_shapes=[pltpu.VMEM((4, cells + 2 * ROW, FF_WIDTH), F32)] * 4
        + [
            pltpu.VMEM((4 * cells, FF_WIDTH), HALF),
            pltpu.VMEM((4 * cells, FF_WIDTH), HALF),
            pltpu.VMEM((4 * cells, width), HALF),
            pltpu.VMEM((4 * cells, width), F32),
        ],
        compiler_params=params(),
        cost_estimate=cost(40e9, 40e6),
    )(arrived, product, normed_two, mixed_two, hidden, pieces, w_fc1, conv_ffn, w_fc2)


def attention_backward(mixed_grad, mixed_one, normed_one, merged, attended, pieces, w_qkv, w_proj):
    _, cells, width = mixed_grad.shape

    def kernel(
        came, mixed, normed, merged, attended, pieces, w_qkv, w_proj,
        one_grad, qkv_grad, proj_grad, vectors, merged_grad, attended_grad, qkv_sum, proj_sum, sums,
    ):
        step = pl.program_id(0)

        @pl.when(step == 0)
        def _():
            qkv_sum[...] = jnp.zeros_like(qkv_sum)
            proj_sum[...] = jnp.zeros_like(proj_sum)
            sums[...] = jnp.zeros_like(sums)

        projected = dot(attended[0], w_proj[...], NN)
        sums[2:3, :] += jnp.sum(came[0] * projected, axis=0, keepdims=True)
        gated = (came[0] * pieces[2:3, :]).astype(HALF)
        proj_sum[...] += dot(attended[0], gated, TN)
        attended_grad[...] = dot(gated, w_proj[...], NT).astype(HALF)
        masks = head_masks(cells)

        def pair(k, carry):
            at = pl.multiple_of(k * 128, 128)
            queries = merged[0, :, pl.ds(at, 128)] * jnp.asarray(0.125, HALF)
            keys = merged[0, :, pl.ds(width + at, 128)]
            values = merged[0, :, pl.ds(2 * width + at, 128)]
            grads = attended_grad[:, pl.ds(at, 128)]
            query_total, key_total, value_total = (None, None, None)
            for mask in masks:
                scores = dot(queries * mask, keys, NT)
                scores = jnp.exp(scores - jnp.max(scores, axis=-1, keepdims=True))
                probs = scores * (1.0 / jnp.sum(scores, axis=-1, keepdims=True))
                masked = grads * mask
                probs_grad = dot(masked, values, NT)
                value_part = dot(probs.astype(HALF), masked, TN)
                along = jnp.sum(probs * probs_grad, axis=-1, keepdims=True)
                scores_grad = (probs * (probs_grad - along)).astype(HALF)
                query_part = dot(scores_grad, keys * mask, NN)
                key_part = dot(scores_grad, queries * mask, TN)
                query_total = query_part if query_total is None else query_total + query_part
                key_total = key_part if key_total is None else key_total + key_part
                value_total = value_part if value_total is None else value_total + value_part
            merged_grad[:, pl.ds(at, 128)] = (query_total * 0.125).astype(HALF)
            merged_grad[:, pl.ds(width + at, 128)] = key_total.astype(HALF)
            merged_grad[:, pl.ds(2 * width + at, 128)] = value_total.astype(HALF)
            return carry

        lax.fori_loop(0, HEADS // 2, pair, 0)
        normed_grad = None
        for k in range(3):
            columns = slice(k * width, (k + 1) * width)
            qkv_sum[:, columns] += dot(normed[0], merged_grad[:, columns], TN)
            term = dot(merged_grad[:, columns], w_qkv[:, columns], NT)
            normed_grad = term if normed_grad is None else normed_grad + term
        unit, scale = normal_parts(mixed[0])
        sums[0:1, :] += jnp.sum(normed_grad, axis=0, keepdims=True)
        sums[1:2, :] += jnp.sum(normed_grad * unit, axis=0, keepdims=True)
        one_grad[0] = came[0] + normal_back(normed_grad * (1.0 + pieces[1:2, :]), unit, scale)

        @pl.when(step == 3)
        def _():
            qkv_grad[...] = qkv_sum[...].astype(HALF)
            proj_grad[...] = proj_sum[...].astype(HALF)
            vectors[...] = sums[0:3, :]

    def group_block(columns):
        return pl.BlockSpec((1, cells, columns), lambda g: (g, 0, 0))

    return pl.pallas_call(
        kernel,
        name="attention_backward",
        grid=(4,),
        in_specs=[group_block(width * k) for k in (1, 1, 1, 3, 1)]
        + [whole(v.shape) for v in (pieces, w_qkv, w_proj)],
        out_specs=[
            group_block(width),
            whole((width, 3 * width)),
            whole((width, width)),
            whole((3, width)),
        ],
        out_shape=[
            jax.ShapeDtypeStruct((4, cells, width), F32),
            jax.ShapeDtypeStruct((width, 3 * width), HALF),
            jax.ShapeDtypeStruct((width, width), HALF),
            jax.ShapeDtypeStruct((3, width), F32),
        ],
        scratch_shapes=[
            pltpu.VMEM((cells, 3 * width), HALF),
            pltpu.VMEM((cells, width), HALF),
            pltpu.VMEM((width, 3 * width), F32),
            pltpu.VMEM((width, width), F32),
            pltpu.VMEM((8, width), F32),
        ],
        compiler_params=params(),
        cost_estimate=cost(24e9, 25e6),
    )(mixed_grad, mixed_one, normed_one, merged, attended, pieces, w_qkv, w_proj)


def entry_backward(one_grad, arrived, conv_block):
    sources, _, part, width = arrived.shape
    cells = sources * part
    wide = 256

    def kernel(grad, arrived, taps, leaving, tap_grad, plain, moved, grad_plain, grad_moved):
        clear_edges(plain, moved)
        clear_edges(grad_plain, grad_moved)

        def fill(row, carry):
            source, start = at_source(row, part // ROW)
            to = pl.multiple_of((row + 1) * ROW, ROW)
            for group in range(4):
                block = arrived[source, group, pl.ds(start, ROW), :].astype(F32)
                place(plain, moved, group, to, slice(None), block)
                block = grad[group, pl.ds(pl.multiple_of(row * ROW, ROW), ROW), :]
                place(grad_plain, grad_moved, group, to, slice(None), block)
            return carry

        lax.fori_loop(0, cells // ROW, fill, 0)
        for lane in range(wide // 128):
            lanes = slice(lane * 128, (lane + 1) * 128)
            flipped = tap_rows(taps, lanes, True)

            def back_step(row, sums):
                at = pl.multiple_of((row + 1) * ROW, ROW)
                source, start = at_source(row, part // ROW)
                sites = read_sites(grad_plain, grad_moved, at, lanes)
                for group in range(4):
                    own = sites[(group // 2, 0, group % 2, False)]
                    leaving[source, group, pl.ds(start, ROW), lanes] = (
                        own + convolve(sites, flipped, group)
                    ).astype(HALF)
                owns = [sites[(g // 2, 0, g % 2, False)] for g in range(4)]
                sites = read_sites(plain, moved, at, lanes)
                sums = list(sums)
                for group in range(4):
                    values = tap_values(sites, group)
                    for k in range(9):
                        both = values[k] * owns[group]
                        sums[k] = sums[k] + (both[:8] + both[8:])
                return tuple(sums)

            start = tuple(jnp.zeros((8, 128), F32) for _ in range(9))
            sums = lax.fori_loop(0, cells // ROW, back_step, start)
            for k in range(9):
                tap_grad[k : k + 1, lanes] = jnp.sum(sums[k], axis=0, keepdims=True)

    return pl.pallas_call(
        kernel,
        name="entry_backward",
        grid=(width // wide,),
        in_specs=[
            pl.BlockSpec((4, cells, wide), lambda k: (0, 0, k)),
            pl.BlockSpec((sources, 4, part, wide), lambda k: (0, 0, 0, k)),
            pl.BlockSpec((9, wide), lambda k: (0, k)),
        ],
        out_specs=[
            pl.BlockSpec((sources, 4, part, wide), lambda k: (0, 0, 0, k)),
            pl.BlockSpec((9, wide), lambda k: (0, k)),
        ],
        out_shape=[
            jax.ShapeDtypeStruct(arrived.shape, HALF),
            jax.ShapeDtypeStruct((9, width), F32),
        ],
        scratch_shapes=[pltpu.VMEM((4, cells + 2 * ROW, wide), F32)] * 4,
        compiler_params=params(),
        cost_estimate=cost(1e9, 8e6),
    )(one_grad, arrived, conv_block)


def order_matrix(dtype=HALF):
    size = 16 * ROW
    row = lax.broadcasted_iota(jnp.int32, (size, size), 0)
    col = lax.broadcasted_iota(jnp.int32, (size, size), 1)
    a, b = row // (8 * ROW), (row // (4 * ROW)) % 2
    down, across, at = (row // (2 * ROW)) % 2, (row // ROW) % 2, row % ROW
    token = (2 * down + a) * (4 * ROW) + 4 * at + 2 * across + b
    return jnp.where(token == col, 1.0, 0.0).astype(dtype)


def gather_patches(images, weight, transposed):
    items, rows, columns, channels = images.shape
    width = weight.shape[0] if transposed else weight.shape[1]
    steps = rows // 4
    part = steps * ROW

    def kernel(images, order, weight, patches, result):
        def arrange(k, carry):
            block = images[0, pl.ds(k * 4, 4)].reshape(16 * ROW, channels)
            block = dot(order[...], block, NN).astype(HALF)
            for ab in range(4):
                for group in range(4):
                    at = (ab * 4 + group) * ROW
                    patches[0, group, pl.ds(pl.multiple_of(k * ROW, ROW), ROW), pl.ds(ab * channels, channels)] = block[
                        at : at + ROW
                    ]
            return carry

        lax.fori_loop(0, steps, arrange, 0)
        for group in range(4):
            result[0, group] = dot(patches[0, group], weight[...], NT if transposed else NN).astype(HALF)

    return pl.pallas_call(
        kernel,
        name="gather_patches",
        grid=(items,),
        in_specs=[
            pl.BlockSpec((1, rows, columns, channels), lambda k: (k, 0, 0, 0)),
            whole((16 * ROW, 16 * ROW)),
            whole(weight.shape),
        ],
        out_specs=[
            pl.BlockSpec((1, 4, part, 4 * channels), lambda k: (k, 0, 0, 0)),
            pl.BlockSpec((1, 4, part, width), lambda k: (k, 0, 0, 0)),
        ],
        out_shape=[
            jax.ShapeDtypeStruct((items, 4, part, 4 * channels), HALF),
            jax.ShapeDtypeStruct((items, 4, part, width), HALF),
        ],
        compiler_params=params(),
        cost_estimate=cost(3.2e9, 12e6),
    )(images, order_matrix(), weight)


def spread_patches(tokens, weight, base, transposed, dtype):
    items, _, part, width = tokens.shape
    _, rows, columns, channels = base.shape
    steps = rows // 4

    def kernel(tokens, order, weight, base, result, product):
        for group in range(4):
            product[group] = dot(tokens[0, group], weight[...], NT if transposed else NN).astype(HALF)

        def arrange(k, carry):
            at = pl.ds(pl.multiple_of(k * ROW, ROW), ROW)
            block = jnp.concatenate(
                [product[group, at, ab * channels : (ab + 1) * channels] for ab in range(4) for group in range(4)], axis=0
            )
            block = dot(order[...], block, TN).reshape(4, columns, channels)
            here = pl.ds(k * 4, 4)
            result[0, here] = (base[0, here].astype(F32) + block).astype(dtype)
            return carry

        lax.fori_loop(0, steps, arrange, 0)

    image = pl.BlockSpec((1, rows, columns, channels), lambda k: (k, 0, 0, 0))
    return pl.pallas_call(
        kernel,
        name="spread_patches",
        grid=(items,),
        in_specs=[
            pl.BlockSpec((1, 4, part, width), lambda k: (k, 0, 0, 0)),
            whole((16 * ROW, 16 * ROW)),
            whole(weight.shape),
            image,
        ],
        out_specs=image,
        out_shape=jax.ShapeDtypeStruct(base.shape, dtype),
        scratch_shapes=[pltpu.VMEM((4, part, 4 * channels), HALF)],
        compiler_params=params(),
        cost_estimate=cost(3.2e9, 12e6),
    )(tokens, order_matrix(), weight, base)


def own_columns(values, index, count):
    width = values.shape[1] // count
    return lax.dynamic_slice_in_dim(values, index * width, width, axis=1)


def modulate_grads(modulation_grad, buckets, time_table, w_modulate):
    dp_count = lax.axis_size("dp")
    dp_index = lax.axis_index("dp")
    every_grad = lax.all_gather(modulation_grad, ("dp", "row"), axis=0, tiled=True)
    every_bucket = lax.all_gather(buckets, "dp", axis=0, tiled=True)
    own_part = own_columns(time_table[every_bucket], dp_index, dp_count).astype(jnp.float32)
    active = jax.nn.silu(own_part).astype(jnp.bfloat16)
    modulate_grad = jnp.einsum("id,if->df", active, every_grad, preferred_element_type=jnp.float32)
    rows = time_table.shape[1] // dp_count
    own_rows = lax.dynamic_slice_in_dim(w_modulate, dp_index * rows, rows, axis=0)
    active_grad = jnp.einsum("if,df->id", every_grad, own_rows, preferred_element_type=jnp.float32)
    sigmoid = jax.nn.sigmoid(own_part)
    embedding_grad = active_grad * sigmoid * (1.0 + own_part * (1.0 - sigmoid))
    selector = (
        lax.iota(jnp.int32, time_table.shape[0])[:, None] == every_bucket[None, :]
    ).astype(jnp.float32)
    table_grad = jnp.matmul(selector, embedding_grad, precision=lax.Precision.HIGHEST)
    return (table_grad, modulate_grad)


def bit_count(size):
    return size.bit_length() - 1


def swap(value, axis_name, bit):
    size = lax.axis_size(axis_name)
    return lax.ppermute(value, axis_name, [(k, k ^ (1 << bit)) for k in range(size)])


def own_bit(axis_name, bit):
    return (lax.axis_index(axis_name) >> bit) & 1


def added(kept, received):
    return (kept.astype(jnp.float32) + received.astype(jnp.float32)).astype(jnp.bfloat16)


def pick(value, index, axis):
    return lax.dynamic_index_in_dim(value, index, axis=axis, keepdims=False)


LANES = 384


def reduce_group(arrays):
    dp_count, row_count = (lax.axis_size("dp"), lax.axis_size("row"))
    core = own_bit("row", 0)
    blocks = []
    for array in arrays:
        columns = array.shape[1] // 2
        kept = lax.dynamic_slice_in_dim(array, core * columns, columns, axis=1)
        sent = lax.dynamic_slice_in_dim(array, (1 - core) * columns, columns, axis=1)
        half = added(kept, swap(sent, "row", 0)).reshape(dp_count, array.shape[0] // dp_count, columns)
        for start in range(0, columns, LANES):
            blocks.append(half[:, :, start : start + LANES])
    joined = jnp.concatenate(blocks, axis=1)
    d_bits = [("dp", bit) for bit in range(bit_count(dp_count))]
    y_bits = [("row", bit) for bit in range(1, bit_count(row_count))]
    orders = [
        y_bits + d_bits,
        d_bits[:2] + y_bits + d_bits[2:],
        d_bits[1:2] + y_bits + d_bits[:1] + d_bits[2:],
    ]
    dims = d_bits[::-1] + y_bits[::-1]
    total = joined.shape[1]
    parts = joined.reshape((2,) * len(dims) + (3, total // 3 // (row_count // 2), LANES))
    values = [pick(parts, k, len(dims)) for k in range(3)]
    left = [list(dims) for _ in range(3)]
    for step in range(len(dims)):
        for k in range(3):
            at = left[k].index(orders[k][step])
            mine = own_bit(*orders[k][step])
            received = swap(pick(values[k], 1 - mine, at), *orders[k][step])
            values[k] = added(pick(values[k], mine, at), received)
            left[k].pop(at)
    result = jnp.stack(values)
    for name, bit in [*y_bits, ("row", 0)]:
        other = swap(result, name, bit)
        mine = own_bit(name, bit)
        result = jnp.stack([jnp.where(mine == 0, result, other), jnp.where(mine == 0, other, result)])
    result = result.reshape(2, total, LANES).astype(jnp.float32)
    outputs, at = ([], 0)
    for array in arrays:
        rows = array.shape[0] // dp_count
        pieces = []
        for side in range(2):
            for k in range(array.shape[1] // 2 // LANES):
                pieces.append(result[side, at + k * rows : at + (k + 1) * rows])
        at += rows * (array.shape[1] // 2 // LANES)
        outputs.append(jnp.concatenate(pieces, axis=1))
    return outputs


def body(
    latents,
    buckets,
    cotangent,
    time_table,
    w_modulate,
    conv_block,
    w_qkv,
    w_proj,
    w_fc1,
    conv_ffn,
    w_fc2,
    w_down,
    w_up,
):
    row_count = lax.axis_size("row")
    row_index = lax.axis_index("row")
    width = w_proj.shape[0]
    taps_block = conv_block.astype(F32)
    taps_ffn = conv_ffn.astype(F32)

    def exchange(tokens):
        return lax.all_to_all(tokens, "row", split_axis=0, concat_axis=0, tiled=True)

    patches, sending = gather_patches(latents, w_down, False)
    arrived = exchange(sending)
    cot_patches, leaving_grad = gather_patches(cotangent, w_up, True)
    arrived_grad = exchange(leaving_grad)
    own_bucket = lax.dynamic_slice_in_dim(buckets, row_index, 1)
    own_embedding = time_table[own_bucket].astype(F32)
    modulation = jnp.matmul(
        jax.nn.silu(own_embedding).astype(HALF), w_modulate, preferred_element_type=F32
    )
    pieces = modulation.reshape(6, width)

    mixed_one, normed_one, merged, attended, mixed_two, normed_two = attention_forward(
        arrived, pieces, taps_block, w_qkv, w_proj
    )
    hidden, product, leaving = ffn_forward(
        normed_two, mixed_two, pieces, w_fc1, taps_ffn, w_fc2, row_count
    )
    returned = exchange(leaving)
    fc1_grad, fc2_grad, ffn_tap_grad, mixed_grad, vectors_two = ffn_backward(
        arrived_grad, product, normed_two, mixed_two, hidden, pieces, w_fc1, taps_ffn, w_fc2
    )
    output = spread_patches(returned, w_up, latents, False, HALF)
    up_grad = jnp.einsum(
        "agtd,agte->de", returned, cot_patches, preferred_element_type=F32
    ).astype(HALF)
    one_grad, qkv_grad, proj_grad, vectors_one = attention_backward(
        mixed_grad, mixed_one, normed_one, merged, attended, pieces, w_qkv, w_proj
    )
    entering_back, block_tap_grad = entry_backward(one_grad, arrived, taps_block)
    entering_grad = exchange(entering_back)
    down_grad = jnp.einsum(
        "agte,agtd->ed", patches, entering_grad, preferred_element_type=F32
    ).astype(HALF)
    latents_grad = spread_patches(entering_grad, w_down, cotangent, True, F32)

    modulation_grad = jnp.concatenate([vectors_one, vectors_two], axis=0).reshape(1, 6 * width)
    table_grad, modulate_grad = modulate_grads(
        modulation_grad.astype(HALF), buckets, time_table, w_modulate
    )
    conv_all = lax.psum(jnp.concatenate([block_tap_grad, ffn_tap_grad], axis=1), ("row", "dp"))
    dp_index = lax.axis_index("dp")
    dp_count = lax.axis_size("dp")
    early = reduce_group([fc1_grad, fc2_grad, up_grad])
    late = reduce_group([qkv_grad, proj_grad, down_grad])
    return (
        output,
        latents_grad,
        table_grad,
        modulate_grad,
        own_columns(conv_all[:, :width], dp_index, dp_count),
        late[0],
        late[1],
        early[0],
        own_columns(conv_all[:, width:], dp_index, dp_count),
        early[1],
        late[2],
        early[2],
    )


def solution(mesh):
    in_specs = (
        P("dp", "row", None, None),
        P("dp"),
        P("dp", "row", None, None),
        P(),
        P(),
        P(),
        P(),
        P(),
        P(),
        P(),
        P(),
        P(),
        P(),
    )
    out_specs = (
        P("dp", "row", None, None),
        P("dp", "row", None, None),
        P(None, "dp"),
        P("dp", None),
        P(None, "dp"),
        P("dp", None),
        P("dp", None),
        P("dp", None),
        P(None, "dp"),
        P("dp", None),
        P("dp", None),
        P("dp", None),
    )
    return jax.shard_map(body, mesh=mesh, in_specs=in_specs, out_specs=out_specs, check_vma=False)
```

```python
import jax
import jax.numpy as jnp
from jax import lax
from jax.experimental import pallas as pl
from jax.experimental.pallas import tpu as pltpu
from jax.sharding import PartitionSpec as P


HEADS = 12
ROW = 16
FF_WIDTH = 256
F32 = jnp.float32
HALF = jnp.bfloat16
NN = (((1,), (0,)), ((), ()))
NT = (((1,), (1,)), ((), ()))
TN = (((0,), (0,)), ((), ()))
VMEM_LIMIT = 60 * 1024 * 1024


def dot(left, right, dims):
    return lax.dot_general(left, right, dims, preferred_element_type=F32)


def params():
    return pltpu.CompilerParams(vmem_limit_bytes=VMEM_LIMIT)


def cost(flops, moved):
    return pl.CostEstimate(flops=int(flops), bytes_accessed=int(moved), transcendentals=0)


def whole(shape):
    zeros = (0,) * len(shape)
    return pl.BlockSpec(shape, lambda *_: zeros)


def shifted(block, odd):
    at = lax.broadcasted_iota(jnp.int32, block.shape, 0)
    if odd:
        return jnp.where(at == 0, 0.0, pltpu.roll(block, 1, 0))
    return jnp.where(at == ROW - 1, 0.0, pltpu.roll(block, ROW - 1, 0))


def clear_edges(plain, moved):
    rows = plain.shape[1]
    zero = jnp.zeros((ROW, plain.shape[2]), plain.dtype)
    for group in range(4):
        for ref in (plain, moved):
            ref[group, pl.ds(0, ROW), :] = zero
            ref[group, pl.ds(rows - ROW, ROW), :] = zero


def place(plain, moved, group, start, lanes, block):
    plain[group, pl.ds(start, ROW), lanes] = block
    moved[group, pl.ds(start, ROW), lanes] = shifted(block, group % 2 == 1)


ROW_SITES = (((1, -1), (0, 0), (1, 0)), ((0, 0), (1, 0), (0, 1)))
COL_SITES = (((1, True), (0, False), (1, False)), ((0, False), (1, False), (0, True)))


def read_sites(plain, moved, start, lanes):
    sites = {}
    for row_group, offset in ((1, -1), (0, 0), (1, 0), (0, 1)):
        for col_group, is_moved in ((0, False), (1, False), (1, True), (0, True)):
            ref = moved if is_moved else plain
            at = pl.multiple_of(start + offset * ROW, ROW)
            sites[row_group, offset, col_group, is_moved] = ref[
                2 * row_group + col_group, pl.ds(at, ROW), lanes
            ]
    return sites


def tap_values(sites, group):
    values = []
    for down in range(3):
        for across in range(3):
            values.append(sites[ROW_SITES[group // 2][down] + COL_SITES[group % 2][across]])
    return values


def convolve(sites, taps, group):
    values = tap_values(sites, group)
    total = values[0] * taps[0]
    for k in range(1, 9):
        total = total + values[k] * taps[k]
    return total


def tap_rows(kernel_ref, lanes, flip):
    return [kernel_ref[pl.ds(8 - k if flip else k, 1), lanes] for k in range(9)]


def normal_parts(values):
    centered = values - jnp.mean(values, axis=-1, keepdims=True)
    scale = lax.rsqrt(jnp.mean(centered * centered, axis=-1, keepdims=True) + 1e-06)
    return centered * scale, scale


def normal_back(grad, unit, scale):
    average = jnp.mean(grad, axis=-1, keepdims=True)
    along = jnp.mean(grad * unit, axis=-1, keepdims=True)
    return scale * (grad - average - unit * along)


def head_masks(rows):
    low_lanes = lax.broadcasted_iota(jnp.int32, (rows, 128), 1) < 64
    first = jnp.where(low_lanes, 1.0, 0.0)
    return first.astype(HALF), (1.0 - first).astype(HALF)


def at_source(row_block, blocks_each):
    return row_block // blocks_each, pl.multiple_of((row_block % blocks_each) * ROW, ROW)


def attention_forward(arrived, pieces, conv_block, w_qkv, w_proj):
    sources, _, part, width = arrived.shape
    cells = sources * part

    def kernel(
        arrived, pieces, taps, w_qkv, w_proj, mixed_one, normed_one, merged, attended, mixed_two, normed_two, plain, moved, mixed
    ):
        step = pl.program_id(0)

        @pl.when(step == 0)
        def _():
            clear_edges(plain, moved)

            def fill(row, carry):
                source, start = at_source(row, part // ROW)
                to = pl.multiple_of((row + 1) * ROW, ROW)
                for group in range(4):
                    block = arrived[source, group, pl.ds(start, ROW), :].astype(F32)
                    place(plain, moved, group, to, slice(None), block)
                return carry

            lax.fori_loop(0, cells // ROW, fill, 0)

            def lane_step(lane, carry):
                lanes = pl.ds(pl.multiple_of(lane * 128, 128), 128)
                rows = tap_rows(taps, lanes, False)

                def conv_step(row, carry):
                    at = pl.multiple_of((row + 1) * ROW, ROW)
                    sites = read_sites(plain, moved, at, lanes)
                    for group in range(4):
                        mixed[group, pl.ds(pl.multiple_of(row * ROW, ROW), ROW), lanes] = sites[
                            (group // 2, 0, group % 2, False)
                        ] + convolve(sites, rows, group)
                    return carry

                return lax.fori_loop(0, cells // ROW, conv_step, carry)

            lax.fori_loop(0, width // 128, lane_step, 0)

        values = mixed[step]
        mixed_one[0] = values
        unit, _ = normal_parts(values)
        normed_one[0] = (unit * (1.0 + pieces[1:2, :]) + pieces[0:1, :]).astype(HALF)
        for k in range(3):
            merged[0, :, k * width : (k + 1) * width] = dot(
                normed_one[0], w_qkv[:, k * width : (k + 1) * width], NN
            ).astype(HALF)
        masks = head_masks(cells)

        def pair(k, carry):
            at = pl.multiple_of(k * 128, 128)
            queries = merged[0, :, pl.ds(at, 128)] * jnp.asarray(0.125, HALF)
            keys = merged[0, :, pl.ds(width + at, 128)]
            values = merged[0, :, pl.ds(2 * width + at, 128)]
            total = None
            for mask in masks:
                scores = dot(queries * mask, keys, NT)
                scores = jnp.exp(scores - jnp.max(scores, axis=-1, keepdims=True))
                share = 1.0 / jnp.sum(scores, axis=-1, keepdims=True)
                result = dot(scores.astype(HALF), values * mask, NN) * share
                total = result if total is None else total + result
            attended[0, :, pl.ds(at, 128)] = total.astype(HALF)
            return carry

        lax.fori_loop(0, HEADS // 2, pair, 0)
        values = mixed[step] + pieces[2:3, :] * dot(attended[0], w_proj[...], NN)
        mixed_two[0] = values
        unit, _ = normal_parts(values)
        normed_two[0] = (unit * (1.0 + pieces[4:5, :]) + pieces[3:4, :]).astype(HALF)

    def group_block(columns):
        return pl.BlockSpec((1, cells, columns), lambda g: (g, 0, 0))

    def array(columns, dtype):
        return jax.ShapeDtypeStruct((4, cells, columns), dtype)

    return pl.pallas_call(
        kernel,
        name="attention_forward",
        grid=(4,),
        in_specs=[whole(v.shape) for v in (arrived, pieces, conv_block, w_qkv, w_proj)],
        out_specs=[group_block(width * k) for k in (1, 1, 3, 1, 1, 1)],
        out_shape=[
            array(width, F32),
            array(width, HALF),
            array(3 * width, HALF),
            array(width, HALF),
            array(width, F32),
            array(width, HALF),
        ],
        scratch_shapes=[
            pltpu.VMEM((4, cells + 2 * ROW, width), F32),
            pltpu.VMEM((4, cells + 2 * ROW, width), F32),
            pltpu.VMEM((4, cells, width), F32),
        ],
        compiler_params=params(),
        cost_estimate=cost(12e9, 25e6),
    )(arrived, pieces, conv_block, w_qkv, w_proj)


def fill_from(plain, moved, group, values):
    cells = values.shape[0]
    plain[group, pl.ds(ROW, cells), :] = values
    at = lax.broadcasted_iota(jnp.int32, values.shape, 0) % ROW
    if group % 2 == 1:
        side = jnp.where(at == 0, 0.0, pltpu.roll(values, 1, 0))
    else:
        side = jnp.where(at == ROW - 1, 0.0, pltpu.roll(values, cells - 1, 0))
    moved[group, pl.ds(ROW, cells), :] = side


ROOT = 0.7978845608028654


def gelu(values):
    return 0.5 * values * (1.0 + jnp.tanh(ROOT * (values + 0.044715 * (values * values * values))))


def gelu_pair(values):
    square = values * values
    bend = jnp.tanh(ROOT * values * (1.0 + 0.044715 * square))
    half = 0.5 * (1.0 + bend)
    slope = half + 0.5 * values * (1.0 - bend * bend) * (ROOT + (3.0 * 0.044715 * ROOT) * square)
    return values * half, slope


def ffn_both(arrived, normed_two, mixed_two, pieces, w_fc1, conv_ffn, w_fc2):
    sources, _, part, width = arrived.shape
    cells = sources * part
    hidden_width = w_fc1.shape[1]
    steps = hidden_width // FF_WIDTH

    def kernel(
        arrived, normed, mixed, pieces, w_one, taps, w_two,
        one_grad, two_grad, tap_grad, mixed_grad, leaving, vectors,
        plain, moved, grad_plain, grad_moved, active, hidden_grad, gated, product, total,
    ):
        step = pl.program_id(0)

        @pl.when(step == 0)
        def _():
            clear_edges(plain, moved)
            clear_edges(grad_plain, grad_moved)
            total[...] = jnp.zeros_like(total)
            product[...] = jnp.zeros_like(product)
            for group in range(4):
                for source in range(sources):
                    to = pl.ds(group * cells + source * part, part)
                    gated[to, :] = (arrived[source, group].astype(F32) * pieces[5:6, :]).astype(HALF)

        for group in range(4):
            fill_from(plain, moved, group, dot(normed[group], w_one[...], NN))
            grad_plain[group, pl.ds(ROW, cells), :] = dot(
                gated[pl.ds(group * cells, cells), :], w_two[...], NT
            )

        for lane in range(FF_WIDTH // 128):
            lanes = slice(lane * 128, (lane + 1) * 128)
            rows = tap_rows(taps, lanes, False)
            flipped = tap_rows(taps, lanes, True)

            def gelu_step(row, sums):
                at = pl.multiple_of((row + 1) * ROW, ROW)
                sites = read_sites(plain, moved, at, lanes)
                sums = list(sums)
                for group in range(4):
                    values = tap_values(sites, group)
                    result, slope = gelu_pair(convolve(sites, rows, group))
                    to = pl.ds(pl.multiple_of(group * cells + row * ROW, ROW), ROW)
                    active[to, lanes] = result.astype(HALF)
                    grad = grad_plain[group, pl.ds(at, ROW), lanes] * slope
                    place(grad_plain, grad_moved, group, at, lanes, grad)
                    for k in range(9):
                        both = values[k] * grad
                        sums[k] = sums[k] + (both[:8] + both[8:])
                return tuple(sums)

            start = tuple(jnp.zeros((8, 128), F32) for _ in range(9))
            sums = lax.fori_loop(0, cells // ROW, gelu_step, start)
            for k in range(9):
                tap_grad[k : k + 1, lanes] = jnp.sum(sums[k], axis=0, keepdims=True)

            def back_step(row, carry):
                at = pl.multiple_of((row + 1) * ROW, ROW)
                sites = read_sites(grad_plain, grad_moved, at, lanes)
                for group in range(4):
                    to = pl.ds(pl.multiple_of(group * cells + row * ROW, ROW), ROW)
                    hidden_grad[to, lanes] = convolve(sites, flipped, group).astype(HALF)
                return carry

            lax.fori_loop(0, cells // ROW, back_step, 0)

        two_grad[...] = dot(active[...], gated[...], TN).astype(HALF)
        product[...] += dot(active[...], w_two[...], NN)
        grads = hidden_grad[...]
        everything = normed[...].reshape(4 * cells, width)
        one_grad[...] = dot(everything, grads, TN).astype(HALF)
        total[...] += dot(grads, w_one[...], NT)

        @pl.when(step == steps - 1)
        def _():
            shift_sum = jnp.zeros((1, width), F32)
            scale_sum = jnp.zeros((1, width), F32)
            gate_sum = jnp.zeros((1, width), F32)
            for group in range(4):
                for source in range(sources):
                    to = pl.ds(source * part, part)
                    here = pl.ds(group * cells + source * part, part)
                    values = mixed[group, to, :]
                    unit, scale = normal_parts(values)
                    grad = total[here, :]
                    came = arrived[source, group].astype(F32)
                    leaving[source, group] = (values + pieces[5:6, :] * product[here, :]).astype(HALF)
                    shift_sum += jnp.sum(grad, axis=0, keepdims=True)
                    scale_sum += jnp.sum(grad * unit, axis=0, keepdims=True)
                    gate_sum += jnp.sum(came * product[here, :], axis=0, keepdims=True)
                    mixed_grad[group, to, :] = came + normal_back(
                        grad * (1.0 + pieces[4:5, :]), unit, scale
                    )
            vectors[0:1, :] = shift_sum
            vectors[1:2, :] = scale_sum
            vectors[2:3, :] = gate_sum

    def once(value):
        zeros = (0,) * value.ndim
        return pl.BlockSpec(value.shape, lambda k: zeros, pipeline_mode=pl.Buffered(1))

    return pl.pallas_call(
        kernel,
        name="ffn_both",
        grid=(steps,),
        in_specs=[
            once(arrived),
            once(normed_two),
            once(mixed_two),
            once(pieces),
            pl.BlockSpec((width, FF_WIDTH), lambda k: (0, k)),
            pl.BlockSpec((9, FF_WIDTH), lambda k: (0, k)),
            pl.BlockSpec((FF_WIDTH, width), lambda k: (k, 0)),
        ],
        out_specs=[
            pl.BlockSpec((width, FF_WIDTH), lambda k: (0, k)),
            pl.BlockSpec((FF_WIDTH, width), lambda k: (k, 0)),
            pl.BlockSpec((9, FF_WIDTH), lambda k: (0, k)),
            whole((4, cells, width)),
            whole(arrived.shape),
            whole((3, width)),
        ],
        out_shape=[
            jax.ShapeDtypeStruct((width, hidden_width), HALF),
            jax.ShapeDtypeStruct((hidden_width, width), HALF),
            jax.ShapeDtypeStruct((9, hidden_width), F32),
            jax.ShapeDtypeStruct((4, cells, width), F32),
            jax.ShapeDtypeStruct(arrived.shape, HALF),
            jax.ShapeDtypeStruct((3, width), F32),
        ],
        scratch_shapes=[pltpu.VMEM((4, cells + 2 * ROW, FF_WIDTH), F32)] * 4
        + [
            pltpu.VMEM((4 * cells, FF_WIDTH), HALF),
            pltpu.VMEM((4 * cells, FF_WIDTH), HALF),
            pltpu.VMEM((4 * cells, width), HALF),
            pltpu.VMEM((4 * cells, width), F32),
            pltpu.VMEM((4 * cells, width), F32),
        ],
        compiler_params=params(),
        cost_estimate=cost(50e9, 40e6),
    )(arrived, normed_two, mixed_two, pieces, w_fc1, conv_ffn, w_fc2)


def attention_backward(mixed_grad, mixed_one, normed_one, merged, attended, pieces, w_qkv, w_proj):
    _, cells, width = mixed_grad.shape

    def kernel(
        came, mixed, normed, merged, attended, pieces, w_qkv, w_proj,
        one_grad, qkv_grad, proj_grad, vectors, merged_grad, attended_grad, qkv_sum, proj_sum, sums,
    ):
        step = pl.program_id(0)

        @pl.when(step == 0)
        def _():
            qkv_sum[...] = jnp.zeros_like(qkv_sum)
            proj_sum[...] = jnp.zeros_like(proj_sum)
            sums[...] = jnp.zeros_like(sums)

        projected = dot(attended[0], w_proj[...], NN)
        sums[2:3, :] += jnp.sum(came[0] * projected, axis=0, keepdims=True)
        gated = (came[0] * pieces[2:3, :]).astype(HALF)
        proj_sum[...] += dot(attended[0], gated, TN)
        attended_grad[...] = dot(gated, w_proj[...], NT).astype(HALF)
        masks = head_masks(cells)

        def pair(k, carry):
            at = pl.multiple_of(k * 128, 128)
            queries = merged[0, :, pl.ds(at, 128)] * jnp.asarray(0.125, HALF)
            keys = merged[0, :, pl.ds(width + at, 128)]
            values = merged[0, :, pl.ds(2 * width + at, 128)]
            grads = attended_grad[:, pl.ds(at, 128)]
            query_total, key_total, value_total = (None, None, None)
            for mask in masks:
                scores = dot(queries * mask, keys, NT)
                scores = jnp.exp(scores - jnp.max(scores, axis=-1, keepdims=True))
                probs = scores * (1.0 / jnp.sum(scores, axis=-1, keepdims=True))
                masked = grads * mask
                probs_grad = dot(masked, values, NT)
                value_part = dot(probs.astype(HALF), masked, TN)
                along = jnp.sum(probs * probs_grad, axis=-1, keepdims=True)
                scores_grad = (probs * (probs_grad - along)).astype(HALF)
                query_part = dot(scores_grad, keys * mask, NN)
                key_part = dot(scores_grad, queries * mask, TN)
                query_total = query_part if query_total is None else query_total + query_part
                key_total = key_part if key_total is None else key_total + key_part
                value_total = value_part if value_total is None else value_total + value_part
            merged_grad[:, pl.ds(at, 128)] = (query_total * 0.125).astype(HALF)
            merged_grad[:, pl.ds(width + at, 128)] = key_total.astype(HALF)
            merged_grad[:, pl.ds(2 * width + at, 128)] = value_total.astype(HALF)
            return carry

        lax.fori_loop(0, HEADS // 2, pair, 0)
        normed_grad = None
        for k in range(3):
            columns = slice(k * width, (k + 1) * width)
            qkv_sum[:, columns] += dot(normed[0], merged_grad[:, columns], TN)
            term = dot(merged_grad[:, columns], w_qkv[:, columns], NT)
            normed_grad = term if normed_grad is None else normed_grad + term
        unit, scale = normal_parts(mixed[0])
        sums[0:1, :] += jnp.sum(normed_grad, axis=0, keepdims=True)
        sums[1:2, :] += jnp.sum(normed_grad * unit, axis=0, keepdims=True)
        one_grad[0] = came[0] + normal_back(normed_grad * (1.0 + pieces[1:2, :]), unit, scale)

        @pl.when(step == 3)
        def _():
            qkv_grad[...] = qkv_sum[...].astype(HALF)
            proj_grad[...] = proj_sum[...].astype(HALF)
            vectors[...] = sums[0:3, :]

    def group_block(columns):
        return pl.BlockSpec((1, cells, columns), lambda g: (g, 0, 0))

    return pl.pallas_call(
        kernel,
        name="attention_backward",
        grid=(4,),
        in_specs=[group_block(width * k) for k in (1, 1, 1, 3, 1)]
        + [whole(v.shape) for v in (pieces, w_qkv, w_proj)],
        out_specs=[
            group_block(width),
            whole((width, 3 * width)),
            whole((width, width)),
            whole((3, width)),
        ],
        out_shape=[
            jax.ShapeDtypeStruct((4, cells, width), F32),
            jax.ShapeDtypeStruct((width, 3 * width), HALF),
            jax.ShapeDtypeStruct((width, width), HALF),
            jax.ShapeDtypeStruct((3, width), F32),
        ],
        scratch_shapes=[
            pltpu.VMEM((cells, 3 * width), HALF),
            pltpu.VMEM((cells, width), HALF),
            pltpu.VMEM((width, 3 * width), F32),
            pltpu.VMEM((width, width), F32),
            pltpu.VMEM((8, width), F32),
        ],
        compiler_params=params(),
        cost_estimate=cost(24e9, 25e6),
    )(mixed_grad, mixed_one, normed_one, merged, attended, pieces, w_qkv, w_proj)


def entry_backward(one_grad, arrived, conv_block):
    sources, _, part, width = arrived.shape
    cells = sources * part
    wide = 256

    def kernel(grad, arrived, taps, leaving, tap_grad, plain, moved, grad_plain, grad_moved):
        clear_edges(plain, moved)
        clear_edges(grad_plain, grad_moved)

        def fill(row, carry):
            source, start = at_source(row, part // ROW)
            to = pl.multiple_of((row + 1) * ROW, ROW)
            for group in range(4):
                block = arrived[source, group, pl.ds(start, ROW), :].astype(F32)
                place(plain, moved, group, to, slice(None), block)
                block = grad[group, pl.ds(pl.multiple_of(row * ROW, ROW), ROW), :]
                place(grad_plain, grad_moved, group, to, slice(None), block)
            return carry

        lax.fori_loop(0, cells // ROW, fill, 0)
        for lane in range(wide // 128):
            lanes = slice(lane * 128, (lane + 1) * 128)
            flipped = tap_rows(taps, lanes, True)

            def back_step(row, sums):
                at = pl.multiple_of((row + 1) * ROW, ROW)
                source, start = at_source(row, part // ROW)
                sites = read_sites(grad_plain, grad_moved, at, lanes)
                for group in range(4):
                    own = sites[(group // 2, 0, group % 2, False)]
                    leaving[source, group, pl.ds(start, ROW), lanes] = (
                        own + convolve(sites, flipped, group)
                    ).astype(HALF)
                owns = [sites[(g // 2, 0, g % 2, False)] for g in range(4)]
                sites = read_sites(plain, moved, at, lanes)
                sums = list(sums)
                for group in range(4):
                    values = tap_values(sites, group)
                    for k in range(9):
                        both = values[k] * owns[group]
                        sums[k] = sums[k] + (both[:8] + both[8:])
                return tuple(sums)

            start = tuple(jnp.zeros((8, 128), F32) for _ in range(9))
            sums = lax.fori_loop(0, cells // ROW, back_step, start)
            for k in range(9):
                tap_grad[k : k + 1, lanes] = jnp.sum(sums[k], axis=0, keepdims=True)

    return pl.pallas_call(
        kernel,
        name="entry_backward",
        grid=(width // wide,),
        in_specs=[
            pl.BlockSpec((4, cells, wide), lambda k: (0, 0, k)),
            pl.BlockSpec((sources, 4, part, wide), lambda k: (0, 0, 0, k)),
            pl.BlockSpec((9, wide), lambda k: (0, k)),
        ],
        out_specs=[
            pl.BlockSpec((sources, 4, part, wide), lambda k: (0, 0, 0, k)),
            pl.BlockSpec((9, wide), lambda k: (0, k)),
        ],
        out_shape=[
            jax.ShapeDtypeStruct(arrived.shape, HALF),
            jax.ShapeDtypeStruct((9, width), F32),
        ],
        scratch_shapes=[pltpu.VMEM((4, cells + 2 * ROW, wide), F32)] * 4,
        compiler_params=params(),
        cost_estimate=cost(1e9, 8e6),
    )(one_grad, arrived, conv_block)


def order_matrix(dtype=HALF):
    size = 16 * ROW
    row = lax.broadcasted_iota(jnp.int32, (size, size), 0)
    col = lax.broadcasted_iota(jnp.int32, (size, size), 1)
    a, b = row // (8 * ROW), (row // (4 * ROW)) % 2
    down, across, at = (row // (2 * ROW)) % 2, (row // ROW) % 2, row % ROW
    token = (2 * down + a) * (4 * ROW) + 4 * at + 2 * across + b
    return jnp.where(token == col, 1.0, 0.0).astype(dtype)


def gather_patches(images, weight, transposed):
    items, rows, columns, channels = images.shape
    width = weight.shape[0] if transposed else weight.shape[1]
    steps = rows // 4
    part = steps * ROW

    def kernel(images, order, weight, patches, result):
        def arrange(k, carry):
            block = images[0, pl.ds(k * 4, 4)].reshape(16 * ROW, channels)
            block = dot(order[...], block, NN).astype(HALF)
            for ab in range(4):
                for group in range(4):
                    at = (ab * 4 + group) * ROW
                    patches[0, group, pl.ds(pl.multiple_of(k * ROW, ROW), ROW), pl.ds(ab * channels, channels)] = block[
                        at : at + ROW
                    ]
            return carry

        lax.fori_loop(0, steps, arrange, 0)
        values = patches[0].reshape(4 * part, 4 * channels)
        values = dot(values, weight[...], NT if transposed else NN).astype(HALF)
        result[0] = values.reshape(4, part, width)

    return pl.pallas_call(
        kernel,
        name="gather_patches",
        grid=(items,),
        in_specs=[
            pl.BlockSpec((1, rows, columns, channels), lambda k: (k, 0, 0, 0)),
            whole((16 * ROW, 16 * ROW)),
            whole(weight.shape),
        ],
        out_specs=[
            pl.BlockSpec((1, 4, part, 4 * channels), lambda k: (k, 0, 0, 0)),
            pl.BlockSpec((1, 4, part, width), lambda k: (k, 0, 0, 0)),
        ],
        out_shape=[
            jax.ShapeDtypeStruct((items, 4, part, 4 * channels), HALF),
            jax.ShapeDtypeStruct((items, 4, part, width), HALF),
        ],
        compiler_params=params(),
        cost_estimate=cost(3.2e9, 12e6),
    )(images, order_matrix(), weight)


def spread_patches(tokens, weight, base, transposed, dtype):
    items, _, part, width = tokens.shape
    _, rows, columns, channels = base.shape
    steps = rows // 4

    def kernel(tokens, order, weight, base, result, product):
        values = dot(tokens[0].reshape(4 * part, width), weight[...], NT if transposed else NN)
        product[...] = values.astype(HALF).reshape(4, part, 4 * channels)

        def arrange(k, carry):
            at = pl.ds(pl.multiple_of(k * ROW, ROW), ROW)
            block = jnp.concatenate(
                [product[group, at, ab * channels : (ab + 1) * channels] for ab in range(4) for group in range(4)], axis=0
            )
            block = dot(order[...], block, TN).reshape(4, columns, channels)
            here = pl.ds(k * 4, 4)
            result[0, here] = (base[0, here].astype(F32) + block).astype(dtype)
            return carry

        lax.fori_loop(0, steps, arrange, 0)

    image = pl.BlockSpec((1, rows, columns, channels), lambda k: (k, 0, 0, 0))
    return pl.pallas_call(
        kernel,
        name="spread_patches",
        grid=(items,),
        in_specs=[
            pl.BlockSpec((1, 4, part, width), lambda k: (k, 0, 0, 0)),
            whole((16 * ROW, 16 * ROW)),
            whole(weight.shape),
            image,
        ],
        out_specs=image,
        out_shape=jax.ShapeDtypeStruct(base.shape, dtype),
        scratch_shapes=[pltpu.VMEM((4, part, 4 * channels), HALF)],
        compiler_params=params(),
        cost_estimate=cost(3.2e9, 12e6),
    )(tokens, order_matrix(), weight, base)


def modulation_forward(bucket, time_table, w_modulate):
    width = time_table.shape[1]
    columns = w_modulate.shape[1]
    block = columns // 6

    def kernel(bucket, table, weight, result):
        row = table[pl.ds(bucket[0] % 8, 1), :].astype(F32)
        row = (row * jax.nn.sigmoid(row)).astype(HALF)
        result[...] = dot(jnp.broadcast_to(row, (8, width)), weight[...], NN)

    return pl.pallas_call(
        kernel,
        name="modulation_forward",
        grid_spec=pltpu.PrefetchScalarGridSpec(
            num_scalar_prefetch=1,
            grid=(6,),
            in_specs=[
                pl.BlockSpec((8, width), lambda k, bucket: (bucket[0] // 8, 0)),
                pl.BlockSpec((width, block), lambda k, bucket: (0, k)),
            ],
            out_specs=pl.BlockSpec((8, block), lambda k, bucket: (0, k)),
        ),
        out_shape=jax.ShapeDtypeStruct((8, columns), F32),
        compiler_params=params(),
        cost_estimate=cost(1e9, 7e6),
    )(bucket, time_table.astype(F32), w_modulate)


def modulation_backward(every_grad, every_bucket, own_table, own_rows):
    items, columns = every_grad.shape
    entries, slice_width = own_table.shape

    def kernel(grads, buckets, table, rows, table_grad, weight_grad):
        at = lax.broadcasted_iota(jnp.int32, (entries, items), 0)
        chosen = jnp.where(at == buckets[...], 1.0, 0.0).astype(HALF)
        embedding = dot(chosen, table[...], TN)
        sigmoid = jax.nn.sigmoid(embedding)
        active = (embedding * sigmoid).astype(HALF)
        weight_grad[...] = dot(active, grads[...], TN)
        active_grad = dot(grads[...], rows[...], NT)
        grad = active_grad * sigmoid * (1.0 + embedding * (1.0 - sigmoid))
        first = grad.astype(HALF)
        second = (grad - first.astype(F32)).astype(HALF)
        table_grad[...] = dot(chosen, first, NN) + dot(chosen, second, NN)

    return pl.pallas_call(
        kernel,
        name="modulation_backward",
        out_shape=[
            jax.ShapeDtypeStruct((entries, slice_width), F32),
            jax.ShapeDtypeStruct((slice_width, columns), F32),
        ],
        compiler_params=params(),
        cost_estimate=cost(1e9, 4e6),
    )(every_grad, every_bucket, own_table, own_rows)


def own_columns(values, index, count):
    width = values.shape[1] // count
    return lax.dynamic_slice_in_dim(values, index * width, width, axis=1)


def bit_count(size):
    return size.bit_length() - 1


def swap(value, axis_name, bit):
    size = lax.axis_size(axis_name)
    return lax.ppermute(value, axis_name, [(k, k ^ (1 << bit)) for k in range(size)])


def own_bit(axis_name, bit):
    return (lax.axis_index(axis_name) >> bit) & 1


def added(kept, received):
    return (kept.astype(jnp.float32) + received.astype(jnp.float32)).astype(jnp.bfloat16)


def pick(value, index, axis):
    return lax.dynamic_index_in_dim(value, index, axis=axis, keepdims=False)


def gather_bits(value, bits):
    for name, bit in bits:
        other = swap(value, name, bit)
        mine = own_bit(name, bit)
        value = jnp.stack([jnp.where(mine == 0, value, other), jnp.where(mine == 0, other, value)])
    return value


LANES = 384


def reduce_group(arrays):
    dp_count, row_count = (lax.axis_size("dp"), lax.axis_size("row"))
    core = own_bit("row", 0)
    blocks = []
    for array in arrays:
        columns = array.shape[1] // 2
        kept = lax.dynamic_slice_in_dim(array, core * columns, columns, axis=1)
        sent = lax.dynamic_slice_in_dim(array, (1 - core) * columns, columns, axis=1)
        half = added(kept, swap(sent, "row", 0)).reshape(dp_count, array.shape[0] // dp_count, columns)
        for start in range(0, columns, LANES):
            blocks.append(half[:, :, start : start + LANES])
    joined = jnp.concatenate(blocks, axis=1)
    d_bits = [("dp", bit) for bit in range(bit_count(dp_count))]
    y_bits = [("row", bit) for bit in range(1, bit_count(row_count))]
    orders = [
        y_bits + d_bits,
        d_bits[:2] + y_bits + d_bits[2:],
        d_bits[1:2] + y_bits + d_bits[:1] + d_bits[2:],
    ]
    dims = d_bits[::-1] + y_bits[::-1]
    total = joined.shape[1]
    parts = joined.reshape((2,) * len(dims) + (3, total // 3 // (row_count // 2), LANES))
    values = [pick(parts, k, len(dims)) for k in range(3)]
    left = [list(dims) for _ in range(3)]
    for step in range(len(dims)):
        for k in range(3):
            at = left[k].index(orders[k][step])
            mine = own_bit(*orders[k][step])
            received = swap(pick(values[k], 1 - mine, at), *orders[k][step])
            values[k] = added(pick(values[k], mine, at), received)
            left[k].pop(at)
    result = jnp.stack(values)
    for name, bit in [*y_bits, ("row", 0)]:
        other = swap(result, name, bit)
        mine = own_bit(name, bit)
        result = jnp.stack([jnp.where(mine == 0, result, other), jnp.where(mine == 0, other, result)])
    result = result.reshape(2, total, LANES).astype(jnp.float32)
    outputs, at = ([], 0)
    for array in arrays:
        rows = array.shape[0] // dp_count
        pieces = []
        for side in range(2):
            for k in range(array.shape[1] // 2 // LANES):
                pieces.append(result[side, at + k * rows : at + (k + 1) * rows])
        at += rows * (array.shape[1] // 2 // LANES)
        outputs.append(jnp.concatenate(pieces, axis=1))
    return outputs


def body(
    latents,
    buckets,
    cotangent,
    time_table,
    w_modulate,
    conv_block,
    w_qkv,
    w_proj,
    w_fc1,
    conv_ffn,
    w_fc2,
    w_down,
    w_up,
):
    row_count = lax.axis_size("row")
    row_index = lax.axis_index("row")
    width = w_proj.shape[0]
    taps_block = conv_block.astype(F32)
    taps_ffn = conv_ffn.astype(F32)

    def exchange(tokens):
        return lax.all_to_all(tokens, "row", split_axis=0, concat_axis=0, tiled=True)

    patches, sending = gather_patches(latents, w_down, False)
    arrived = exchange(sending)
    cot_patches, leaving_grad = gather_patches(cotangent, w_up, True)
    arrived_grad = exchange(leaving_grad)
    own_bucket = lax.dynamic_slice_in_dim(buckets, row_index, 1)
    pieces = modulation_forward(own_bucket, time_table, w_modulate)[0].reshape(6, width)
    row_bits = [("row", bit) for bit in range(bit_count(row_count))]
    dp_bits = [("dp", bit) for bit in range(bit_count(lax.axis_size("dp")))]
    every_bucket = gather_bits(buckets, dp_bits).reshape(1, -1)

    mixed_one, normed_one, merged, attended, mixed_two, normed_two = attention_forward(
        arrived, pieces, taps_block, w_qkv, w_proj
    )
    fc1_grad, fc2_grad, ffn_tap_grad, mixed_grad, leaving, vectors_two = ffn_both(
        arrived_grad, normed_two, mixed_two, pieces, w_fc1, taps_ffn, w_fc2
    )
    returned = exchange(leaving)
    output = spread_patches(returned, w_up, latents, False, HALF)
    up_grad = jnp.einsum(
        "agtd,agte->de", returned, cot_patches, preferred_element_type=F32
    ).astype(HALF)
    one_grad, qkv_grad, proj_grad, vectors_one = attention_backward(
        mixed_grad, mixed_one, normed_one, merged, attended, pieces, w_qkv, w_proj
    )
    entering_back, block_tap_grad = entry_backward(one_grad, arrived, taps_block)
    entering_grad = exchange(entering_back)
    down_grad = jnp.einsum(
        "agte,agtd->ed", patches, entering_grad, preferred_element_type=F32
    ).astype(HALF)
    latents_grad = spread_patches(entering_grad, w_down, cotangent, True, F32)

    modulation_grad = jnp.concatenate([vectors_one, vectors_two], axis=0).reshape(6 * width)
    every_grad = gather_bits(modulation_grad.astype(HALF), row_bits + dp_bits).reshape(-1, 6 * width)
    dp_index = lax.axis_index("dp")
    dp_count = lax.axis_size("dp")
    rows = width // dp_count
    table_grad, modulate_grad = modulation_backward(
        every_grad,
        every_bucket,
        own_columns(time_table, dp_index, dp_count),
        lax.dynamic_slice_in_dim(w_modulate, dp_index * rows, rows, axis=0),
    )
    ffn_columns = conv_ffn.shape[1] // dp_count
    tap_grads = jnp.concatenate(
        [ffn_tap_grad.reshape(9, dp_count, -1), block_tap_grad.reshape(9, dp_count, -1)], axis=2
    ).transpose(1, 0, 2)
    tap_grads = jnp.pad(tap_grads, ((0, 0), (0, 39), (0, 2 * LANES - tap_grads.shape[2])))
    tap_grads = tap_grads.reshape(48 * dp_count, 2 * LANES).astype(HALF)
    early = reduce_group([fc1_grad, fc2_grad, up_grad])
    late = reduce_group([qkv_grad, proj_grad, down_grad, tap_grads])
    return (
        output,
        latents_grad,
        table_grad,
        modulate_grad,
        late[3][:9, ffn_columns : ffn_columns + rows],
        late[0],
        late[1],
        early[0],
        late[3][:9, :ffn_columns],
        early[1],
        late[2],
        early[2],
    )


def solution(mesh):
    in_specs = (
        P("dp", "row", None, None),
        P("dp"),
        P("dp", "row", None, None),
        P(),
        P(),
        P(),
        P(),
        P(),
        P(),
        P(),
        P(),
        P(),
        P(),
    )
    out_specs = (
        P("dp", "row", None, None),
        P("dp", "row", None, None),
        P(None, "dp"),
        P("dp", None),
        P(None, "dp"),
        P("dp", None),
        P("dp", None),
        P("dp", None),
        P(None, "dp"),
        P("dp", None),
        P("dp", None),
        P("dp", None),
    )
    return jax.shard_map(body, mesh=mesh, in_specs=in_specs, out_specs=out_specs, check_vma=False)
```

```python
import jax
import jax.numpy as jnp
from jax import lax
from jax.experimental import pallas as pl
from jax.experimental.pallas import tpu as pltpu
from jax.sharding import PartitionSpec as P


HEADS = 12
ROW = 16
FF_WIDTH = 256
F32 = jnp.float32
HALF = jnp.bfloat16
NN = (((1,), (0,)), ((), ()))
NT = (((1,), (1,)), ((), ()))
TN = (((0,), (0,)), ((), ()))
VMEM_LIMIT = 60 * 1024 * 1024


def dot(left, right, dims):
    return lax.dot_general(left, right, dims, preferred_element_type=F32)


def params():
    return pltpu.CompilerParams(vmem_limit_bytes=VMEM_LIMIT)


def cost(flops, moved):
    return pl.CostEstimate(flops=int(flops), bytes_accessed=int(moved), transcendentals=0)


def whole(shape):
    zeros = (0,) * len(shape)
    return pl.BlockSpec(shape, lambda *_: zeros)


def shifted(block, odd):
    at = lax.broadcasted_iota(jnp.int32, block.shape, 0)
    if odd:
        return jnp.where(at == 0, 0.0, pltpu.roll(block, 1, 0))
    return jnp.where(at == ROW - 1, 0.0, pltpu.roll(block, ROW - 1, 0))


def clear_edges(plain, moved):
    rows = plain.shape[1]
    zero = jnp.zeros((ROW, plain.shape[2]), plain.dtype)
    for group in range(4):
        for ref in (plain, moved):
            ref[group, pl.ds(0, ROW), :] = zero
            ref[group, pl.ds(rows - ROW, ROW), :] = zero


def place(plain, moved, group, start, lanes, block):
    plain[group, pl.ds(start, ROW), lanes] = block
    moved[group, pl.ds(start, ROW), lanes] = shifted(block, group % 2 == 1)


ROW_SITES = (((1, -1), (0, 0), (1, 0)), ((0, 0), (1, 0), (0, 1)))
COL_SITES = (((1, True), (0, False), (1, False)), ((0, False), (1, False), (0, True)))


def read_sites(plain, moved, start, lanes):
    sites = {}
    for row_group, offset in ((1, -1), (0, 0), (1, 0), (0, 1)):
        for col_group, is_moved in ((0, False), (1, False), (1, True), (0, True)):
            ref = moved if is_moved else plain
            at = pl.multiple_of(start + offset * ROW, ROW)
            sites[row_group, offset, col_group, is_moved] = ref[
                2 * row_group + col_group, pl.ds(at, ROW), lanes
            ]
    return sites


def tap_values(sites, group):
    values = []
    for down in range(3):
        for across in range(3):
            values.append(sites[ROW_SITES[group // 2][down] + COL_SITES[group % 2][across]])
    return values


def convolve(sites, taps, group):
    values = tap_values(sites, group)
    total = values[0] * taps[0]
    for k in range(1, 9):
        total = total + values[k] * taps[k]
    return total


def tap_rows(kernel_ref, lanes, flip):
    return [kernel_ref[pl.ds(8 - k if flip else k, 1), lanes] for k in range(9)]


def normal_parts(values):
    centered = values - jnp.mean(values, axis=-1, keepdims=True)
    scale = lax.rsqrt(jnp.mean(centered * centered, axis=-1, keepdims=True) + 1e-06)
    return centered * scale, scale


def normal_back(grad, unit, scale):
    average = jnp.mean(grad, axis=-1, keepdims=True)
    along = jnp.mean(grad * unit, axis=-1, keepdims=True)
    return scale * (grad - average - unit * along)


def head_masks(rows):
    low_lanes = lax.broadcasted_iota(jnp.int32, (rows, 128), 1) < 64
    first = jnp.where(low_lanes, 1.0, 0.0)
    return first.astype(HALF), (1.0 - first).astype(HALF)


def at_source(row_block, blocks_each):
    return row_block // blocks_each, pl.multiple_of((row_block % blocks_each) * ROW, ROW)


def attention_forward(arrived, pieces, conv_block, w_qkv, w_proj):
    sources, _, part, width = arrived.shape
    cells = sources * part

    def kernel(
        arrived, pieces, taps, w_qkv, w_proj, mixed_one, normed_one, merged, attended, mixed_two, normed_two, plain, moved, mixed
    ):
        step = pl.program_id(0)

        @pl.when(step == 0)
        def _():
            clear_edges(plain, moved)

            def fill(row, carry):
                source, start = at_source(row, part // ROW)
                to = pl.multiple_of((row + 1) * ROW, ROW)
                for group in range(4):
                    block = arrived[source, group, pl.ds(start, ROW), :].astype(F32)
                    place(plain, moved, group, to, slice(None), block)
                return carry

            lax.fori_loop(0, cells // ROW, fill, 0)

            def lane_step(lane, carry):
                lanes = pl.ds(pl.multiple_of(lane * 128, 128), 128)
                rows = tap_rows(taps, lanes, False)

                def conv_step(row, carry):
                    at = pl.multiple_of((row + 1) * ROW, ROW)
                    sites = read_sites(plain, moved, at, lanes)
                    for group in range(4):
                        mixed[group, pl.ds(pl.multiple_of(row * ROW, ROW), ROW), lanes] = sites[
                            (group // 2, 0, group % 2, False)
                        ] + convolve(sites, rows, group)
                    return carry

                return lax.fori_loop(0, cells // ROW, conv_step, carry)

            lax.fori_loop(0, width // 128, lane_step, 0)

        values = mixed[step]
        mixed_one[0] = values
        unit, _ = normal_parts(values)
        normed_one[0] = (unit * (1.0 + pieces[1:2, :]) + pieces[0:1, :]).astype(HALF)
        for k in range(3):
            merged[0, :, k * width : (k + 1) * width] = dot(
                normed_one[0], w_qkv[:, k * width : (k + 1) * width], NN
            ).astype(HALF)
        masks = head_masks(cells)

        def pair(k, carry):
            at = pl.multiple_of(k * 128, 128)
            queries = merged[0, :, pl.ds(at, 128)] * jnp.asarray(0.125, HALF)
            keys = merged[0, :, pl.ds(width + at, 128)]
            values = merged[0, :, pl.ds(2 * width + at, 128)]
            total = None
            for mask in masks:
                scores = dot(queries * mask, keys, NT)
                scores = jnp.exp(scores - jnp.max(scores, axis=-1, keepdims=True))
                share = 1.0 / jnp.sum(scores, axis=-1, keepdims=True)
                result = dot(scores.astype(HALF), values * mask, NN) * share
                total = result if total is None else total + result
            attended[0, :, pl.ds(at, 128)] = total.astype(HALF)
            return carry

        lax.fori_loop(0, HEADS // 2, pair, 0)
        values = mixed[step] + pieces[2:3, :] * dot(attended[0], w_proj[...], NN)
        mixed_two[0] = values
        unit, _ = normal_parts(values)
        normed_two[0] = (unit * (1.0 + pieces[4:5, :]) + pieces[3:4, :]).astype(HALF)

    def group_block(columns):
        return pl.BlockSpec((1, cells, columns), lambda g: (g, 0, 0))

    def array(columns, dtype):
        return jax.ShapeDtypeStruct((4, cells, columns), dtype)

    return pl.pallas_call(
        kernel,
        name="attention_forward",
        grid=(4,),
        in_specs=[whole(v.shape) for v in (arrived, pieces, conv_block, w_qkv, w_proj)],
        out_specs=[group_block(width * k) for k in (1, 1, 3, 1, 1, 1)],
        out_shape=[
            array(width, F32),
            array(width, HALF),
            array(3 * width, HALF),
            array(width, HALF),
            array(width, F32),
            array(width, HALF),
        ],
        scratch_shapes=[
            pltpu.VMEM((4, cells + 2 * ROW, width), F32),
            pltpu.VMEM((4, cells + 2 * ROW, width), F32),
            pltpu.VMEM((4, cells, width), F32),
        ],
        compiler_params=params(),
        cost_estimate=cost(12e9, 25e6),
    )(arrived, pieces, conv_block, w_qkv, w_proj)


def fill_from(plain, moved, group, values):
    cells = values.shape[0]
    plain[group, pl.ds(ROW, cells), :] = values
    at = lax.broadcasted_iota(jnp.int32, values.shape, 0) % ROW
    if group % 2 == 1:
        side = jnp.where(at == 0, 0.0, pltpu.roll(values, 1, 0))
    else:
        side = jnp.where(at == ROW - 1, 0.0, pltpu.roll(values, cells - 1, 0))
    moved[group, pl.ds(ROW, cells), :] = side


ROOT = 0.7978845608028654


def gelu(values):
    return 0.5 * values * (1.0 + jnp.tanh(ROOT * (values + 0.044715 * (values * values * values))))


def gelu_pair(values):
    square = values * values
    bend = jnp.tanh(ROOT * values * (1.0 + 0.044715 * square))
    half = 0.5 * (1.0 + bend)
    slope = half + 0.5 * values * (1.0 - bend * bend) * (ROOT + (3.0 * 0.044715 * ROOT) * square)
    return values * half, slope


def is_split(width, hidden_width, count):
    return (width // count) % 32 == 0 and hidden_width % (128 * count) == 0


def ffn_both(arrived, normed_two, mixed_two, pieces, w_fc1, conv_ffn, w_fc2, count):
    sources, _, part, width = arrived.shape
    cells = sources * part
    hidden_width = w_fc1.shape[1]
    steps = hidden_width // FF_WIDTH
    slab = width // count // 2
    split = is_split(width, hidden_width, count)
    if split:
        one_spec = pl.BlockSpec((count, 1, 2, slab, FF_WIDTH), lambda k: (0, k, 0, 0, 0))
        one_shape = (count, steps, 2, slab, FF_WIDTH)
        two_spec = pl.BlockSpec((2, 2, 64 * (width // 256), 256), lambda k: (k, 0, 0, 0))
        two_shape = (hidden_width // 128, 2, 64 * (width // 256), 256)
    else:
        one_spec = pl.BlockSpec((width, FF_WIDTH), lambda k: (0, k))
        one_shape = (width, hidden_width)
        two_spec = pl.BlockSpec((FF_WIDTH, width), lambda k: (k, 0))
        two_shape = (hidden_width, width)

    def kernel(
        arrived, normed, mixed, pieces, w_one, taps, w_two,
        one_grad, two_grad, tap_grad, mixed_grad, leaving, vectors,
        plain, moved, grad_plain, grad_moved, active, hidden_grad, gated, product, total,
    ):
        step = pl.program_id(0)

        @pl.when(step == 0)
        def _():
            clear_edges(plain, moved)
            clear_edges(grad_plain, grad_moved)
            total[...] = jnp.zeros_like(total)
            product[...] = jnp.zeros_like(product)
            for group in range(4):
                for source in range(sources):
                    to = pl.ds(group * cells + source * part, part)
                    gated[to, :] = (arrived[source, group].astype(F32) * pieces[5:6, :]).astype(HALF)

        for group in range(4):
            fill_from(plain, moved, group, dot(normed[group], w_one[...], NN))
            grad_plain[group, pl.ds(ROW, cells), :] = dot(
                gated[pl.ds(group * cells, cells), :], w_two[...], NT
            )

        for lane in range(FF_WIDTH // 128):
            lanes = slice(lane * 128, (lane + 1) * 128)
            rows = tap_rows(taps, lanes, False)
            flipped = tap_rows(taps, lanes, True)

            def gelu_step(row, sums):
                at = pl.multiple_of((row + 1) * ROW, ROW)
                sites = read_sites(plain, moved, at, lanes)
                sums = list(sums)
                for group in range(4):
                    values = tap_values(sites, group)
                    result, slope = gelu_pair(convolve(sites, rows, group))
                    to = pl.ds(pl.multiple_of(group * cells + row * ROW, ROW), ROW)
                    active[to, lanes] = result.astype(HALF)
                    grad = grad_plain[group, pl.ds(at, ROW), lanes] * slope
                    place(grad_plain, grad_moved, group, at, lanes, grad)
                    for k in range(9):
                        both = values[k] * grad
                        sums[k] = sums[k] + (both[:8] + both[8:])
                return tuple(sums)

            start = tuple(jnp.zeros((8, 128), F32) for _ in range(9))
            sums = lax.fori_loop(0, cells // ROW, gelu_step, start)
            for k in range(9):
                tap_grad[k : k + 1, lanes] = jnp.sum(sums[k], axis=0, keepdims=True)

            def back_step(row, carry):
                at = pl.multiple_of((row + 1) * ROW, ROW)
                sites = read_sites(grad_plain, grad_moved, at, lanes)
                for group in range(4):
                    to = pl.ds(pl.multiple_of(group * cells + row * ROW, ROW), ROW)
                    hidden_grad[to, lanes] = convolve(sites, flipped, group).astype(HALF)
                return carry

            lax.fori_loop(0, cells // ROW, back_step, 0)

        values = dot(active[...], gated[...], TN).astype(HALF)
        if split:
            for block in range(2):
                for core in range(2):
                    at = block * 128 + core * 64
                    for side in range(width // 256):
                        two_grad[block, core, side * 64 : (side + 1) * 64, :] = values[
                            at : at + 64, side * 256 : (side + 1) * 256
                        ]
        else:
            two_grad[...] = values
        product[...] += dot(active[...], w_two[...], NN)
        grads = hidden_grad[...]
        everything = normed[...].reshape(4 * cells, width)
        values = dot(everything, grads, TN).astype(HALF)
        if split:
            one_grad[:, 0] = values.reshape(count, 2, slab, FF_WIDTH)
        else:
            one_grad[...] = values
        total[...] += dot(grads, w_one[...], NT)

        @pl.when(step == steps - 1)
        def _():
            shift_sum = jnp.zeros((1, width), F32)
            scale_sum = jnp.zeros((1, width), F32)
            gate_sum = jnp.zeros((1, width), F32)
            for group in range(4):
                for source in range(sources):
                    to = pl.ds(source * part, part)
                    here = pl.ds(group * cells + source * part, part)
                    values = mixed[group, to, :]
                    unit, scale = normal_parts(values)
                    grad = total[here, :]
                    came = arrived[source, group].astype(F32)
                    leaving[source, group] = (values + pieces[5:6, :] * product[here, :]).astype(HALF)
                    shift_sum += jnp.sum(grad, axis=0, keepdims=True)
                    scale_sum += jnp.sum(grad * unit, axis=0, keepdims=True)
                    gate_sum += jnp.sum(came * product[here, :], axis=0, keepdims=True)
                    mixed_grad[group, to, :] = came + normal_back(
                        grad * (1.0 + pieces[4:5, :]), unit, scale
                    )
            vectors[0:1, :] = shift_sum
            vectors[1:2, :] = scale_sum
            vectors[2:3, :] = gate_sum

    def once(value):
        zeros = (0,) * value.ndim
        return pl.BlockSpec(value.shape, lambda k: zeros, pipeline_mode=pl.Buffered(1))

    return pl.pallas_call(
        kernel,
        name="ffn_both",
        grid=(steps,),
        in_specs=[
            once(arrived),
            once(normed_two),
            once(mixed_two),
            once(pieces),
            pl.BlockSpec((width, FF_WIDTH), lambda k: (0, k)),
            pl.BlockSpec((9, FF_WIDTH), lambda k: (0, k)),
            pl.BlockSpec((FF_WIDTH, width), lambda k: (k, 0)),
        ],
        out_specs=[
            one_spec,
            two_spec,
            pl.BlockSpec((9, FF_WIDTH), lambda k: (0, k)),
            whole((4, cells, width)),
            whole(arrived.shape),
            whole((3, width)),
        ],
        out_shape=[
            jax.ShapeDtypeStruct(one_shape, HALF),
            jax.ShapeDtypeStruct(two_shape, HALF),
            jax.ShapeDtypeStruct((9, hidden_width), F32),
            jax.ShapeDtypeStruct((4, cells, width), F32),
            jax.ShapeDtypeStruct(arrived.shape, HALF),
            jax.ShapeDtypeStruct((3, width), F32),
        ],
        scratch_shapes=[pltpu.VMEM((4, cells + 2 * ROW, FF_WIDTH), F32)] * 4
        + [
            pltpu.VMEM((4 * cells, FF_WIDTH), HALF),
            pltpu.VMEM((4 * cells, FF_WIDTH), HALF),
            pltpu.VMEM((4 * cells, width), HALF),
            pltpu.VMEM((4 * cells, width), F32),
            pltpu.VMEM((4 * cells, width), F32),
        ],
        compiler_params=params(),
        cost_estimate=cost(50e9, 40e6),
    )(arrived, normed_two, mixed_two, pieces, w_fc1, conv_ffn, w_fc2)


def attention_backward(mixed_grad, mixed_one, normed_one, merged, attended, pieces, w_qkv, w_proj, count, split):
    _, cells, width = mixed_grad.shape
    rows = width // count // 2
    grad_shape = (count, 8, 2, rows, 384) if split else (width, 4 * width)

    def kernel(
        came, mixed, normed, merged, attended, pieces, w_qkv, w_proj,
        one_grad, both_grad, vectors, merged_grad, attended_grad, qkv_sum, proj_sum, sums,
    ):
        step = pl.program_id(0)

        @pl.when(step == 0)
        def _():
            qkv_sum[...] = jnp.zeros_like(qkv_sum)
            proj_sum[...] = jnp.zeros_like(proj_sum)
            sums[...] = jnp.zeros_like(sums)

        projected = dot(attended[0], w_proj[...], NN)
        sums[2:3, :] += jnp.sum(came[0] * projected, axis=0, keepdims=True)
        gated = (came[0] * pieces[2:3, :]).astype(HALF)
        proj_sum[...] += dot(attended[0], gated, TN)
        attended_grad[...] = dot(gated, w_proj[...], NT).astype(HALF)
        masks = head_masks(cells)

        def pair(k, carry):
            at = pl.multiple_of(k * 128, 128)
            queries = merged[0, :, pl.ds(at, 128)] * jnp.asarray(0.125, HALF)
            keys = merged[0, :, pl.ds(width + at, 128)]
            values = merged[0, :, pl.ds(2 * width + at, 128)]
            grads = attended_grad[:, pl.ds(at, 128)]
            query_total, key_total, value_total = (None, None, None)
            for mask in masks:
                scores = dot(queries * mask, keys, NT)
                scores = jnp.exp(scores - jnp.max(scores, axis=-1, keepdims=True))
                probs = scores * (1.0 / jnp.sum(scores, axis=-1, keepdims=True))
                masked = grads * mask
                probs_grad = dot(masked, values, NT)
                value_part = dot(probs.astype(HALF), masked, TN)
                along = jnp.sum(probs * probs_grad, axis=-1, keepdims=True)
                scores_grad = (probs * (probs_grad - along)).astype(HALF)
                query_part = dot(scores_grad, keys * mask, NN)
                key_part = dot(scores_grad, queries * mask, TN)
                query_total = query_part if query_total is None else query_total + query_part
                key_total = key_part if key_total is None else key_total + key_part
                value_total = value_part if value_total is None else value_total + value_part
            merged_grad[:, pl.ds(at, 128)] = (query_total * 0.125).astype(HALF)
            merged_grad[:, pl.ds(width + at, 128)] = key_total.astype(HALF)
            merged_grad[:, pl.ds(2 * width + at, 128)] = value_total.astype(HALF)
            return carry

        lax.fori_loop(0, HEADS // 2, pair, 0)
        normed_grad = None
        for k in range(3):
            columns = slice(k * width, (k + 1) * width)
            qkv_sum[:, columns] += dot(normed[0], merged_grad[:, columns], TN)
            term = dot(merged_grad[:, columns], w_qkv[:, columns], NT)
            normed_grad = term if normed_grad is None else normed_grad + term
        unit, scale = normal_parts(mixed[0])
        sums[0:1, :] += jnp.sum(normed_grad, axis=0, keepdims=True)
        sums[1:2, :] += jnp.sum(normed_grad * unit, axis=0, keepdims=True)
        one_grad[0] = came[0] + normal_back(normed_grad * (1.0 + pieces[1:2, :]), unit, scale)

        @pl.when(step == 3)
        def _():
            for k in range(8):
                if k < 6:
                    values = qkv_sum[:, k * 384 : (k + 1) * 384].astype(HALF)
                else:
                    values = proj_sum[:, (k - 6) * 384 : (k - 5) * 384].astype(HALF)
                if split:
                    both_grad[:, k] = values.reshape(count, 2, rows, 384)
                else:
                    both_grad[:, k * 384 : (k + 1) * 384] = values
            vectors[...] = sums[0:3, :]

    def group_block(columns):
        return pl.BlockSpec((1, cells, columns), lambda g: (g, 0, 0))

    return pl.pallas_call(
        kernel,
        name="attention_backward",
        grid=(4,),
        in_specs=[group_block(width * k) for k in (1, 1, 1, 3, 1)]
        + [whole(v.shape) for v in (pieces, w_qkv, w_proj)],
        out_specs=[
            group_block(width),
            whole(grad_shape),
            whole((3, width)),
        ],
        out_shape=[
            jax.ShapeDtypeStruct((4, cells, width), F32),
            jax.ShapeDtypeStruct(grad_shape, HALF),
            jax.ShapeDtypeStruct((3, width), F32),
        ],
        scratch_shapes=[
            pltpu.VMEM((cells, 3 * width), HALF),
            pltpu.VMEM((cells, width), HALF),
            pltpu.VMEM((width, 3 * width), F32),
            pltpu.VMEM((width, width), F32),
            pltpu.VMEM((8, width), F32),
        ],
        compiler_params=params(),
        cost_estimate=cost(24e9, 25e6),
    )(mixed_grad, mixed_one, normed_one, merged, attended, pieces, w_qkv, w_proj)


def entry_backward(one_grad, arrived, conv_block):
    sources, _, part, width = arrived.shape
    cells = sources * part
    wide = 256

    def kernel(grad, arrived, taps, leaving, tap_grad, plain, moved, grad_plain, grad_moved):
        clear_edges(plain, moved)
        clear_edges(grad_plain, grad_moved)

        def fill(row, carry):
            source, start = at_source(row, part // ROW)
            to = pl.multiple_of((row + 1) * ROW, ROW)
            for group in range(4):
                block = arrived[source, group, pl.ds(start, ROW), :].astype(F32)
                place(plain, moved, group, to, slice(None), block)
                block = grad[group, pl.ds(pl.multiple_of(row * ROW, ROW), ROW), :]
                place(grad_plain, grad_moved, group, to, slice(None), block)
            return carry

        lax.fori_loop(0, cells // ROW, fill, 0)
        for lane in range(wide // 128):
            lanes = slice(lane * 128, (lane + 1) * 128)
            flipped = tap_rows(taps, lanes, True)

            def back_step(row, sums):
                at = pl.multiple_of((row + 1) * ROW, ROW)
                source, start = at_source(row, part // ROW)
                sites = read_sites(grad_plain, grad_moved, at, lanes)
                for group in range(4):
                    own = sites[(group // 2, 0, group % 2, False)]
                    leaving[source, group, pl.ds(start, ROW), lanes] = (
                        own + convolve(sites, flipped, group)
                    ).astype(HALF)
                owns = [sites[(g // 2, 0, g % 2, False)] for g in range(4)]
                sites = read_sites(plain, moved, at, lanes)
                sums = list(sums)
                for group in range(4):
                    values = tap_values(sites, group)
                    for k in range(9):
                        both = values[k] * owns[group]
                        sums[k] = sums[k] + (both[:8] + both[8:])
                return tuple(sums)

            start = tuple(jnp.zeros((8, 128), F32) for _ in range(9))
            sums = lax.fori_loop(0, cells // ROW, back_step, start)
            for k in range(9):
                tap_grad[k : k + 1, lanes] = jnp.sum(sums[k], axis=0, keepdims=True)

    return pl.pallas_call(
        kernel,
        name="entry_backward",
        grid=(width // wide,),
        in_specs=[
            pl.BlockSpec((4, cells, wide), lambda k: (0, 0, k)),
            pl.BlockSpec((sources, 4, part, wide), lambda k: (0, 0, 0, k)),
            pl.BlockSpec((9, wide), lambda k: (0, k)),
        ],
        out_specs=[
            pl.BlockSpec((sources, 4, part, wide), lambda k: (0, 0, 0, k)),
            pl.BlockSpec((9, wide), lambda k: (0, k)),
        ],
        out_shape=[
            jax.ShapeDtypeStruct(arrived.shape, HALF),
            jax.ShapeDtypeStruct((9, width), F32),
        ],
        scratch_shapes=[pltpu.VMEM((4, cells + 2 * ROW, wide), F32)] * 4,
        compiler_params=params(),
        cost_estimate=cost(1e9, 8e6),
    )(one_grad, arrived, conv_block)


def order_matrix(dtype=HALF):
    size = 16 * ROW
    row = lax.broadcasted_iota(jnp.int32, (size, size), 0)
    col = lax.broadcasted_iota(jnp.int32, (size, size), 1)
    a, b = row // (8 * ROW), (row // (4 * ROW)) % 2
    down, across, at = (row // (2 * ROW)) % 2, (row // ROW) % 2, row % ROW
    token = (2 * down + a) * (4 * ROW) + 4 * at + 2 * across + b
    return jnp.where(token == col, 1.0, 0.0).astype(dtype)


def gather_patches(images, weight, transposed):
    items, rows, columns, channels = images.shape
    width = weight.shape[0] if transposed else weight.shape[1]
    steps = rows // 4
    part = steps * ROW

    def kernel(images, order, weight, patches, result):
        def arrange(k, carry):
            block = images[0, pl.ds(k * 4, 4)].reshape(16 * ROW, channels)
            block = dot(order[...], block, NN).astype(HALF)
            for ab in range(4):
                for group in range(4):
                    at = (ab * 4 + group) * ROW
                    patches[0, group, pl.ds(pl.multiple_of(k * ROW, ROW), ROW), pl.ds(ab * channels, channels)] = block[
                        at : at + ROW
                    ]
            return carry

        lax.fori_loop(0, steps, arrange, 0)
        values = patches[0].reshape(4 * part, 4 * channels)
        values = dot(values, weight[...], NT if transposed else NN).astype(HALF)
        result[0] = values.reshape(4, part, width)

    return pl.pallas_call(
        kernel,
        name="gather_patches",
        grid=(items,),
        in_specs=[
            pl.BlockSpec((1, rows, columns, channels), lambda k: (k, 0, 0, 0)),
            whole((16 * ROW, 16 * ROW)),
            whole(weight.shape),
        ],
        out_specs=[
            pl.BlockSpec((1, 4, part, 4 * channels), lambda k: (k, 0, 0, 0)),
            pl.BlockSpec((1, 4, part, width), lambda k: (k, 0, 0, 0)),
        ],
        out_shape=[
            jax.ShapeDtypeStruct((items, 4, part, 4 * channels), HALF),
            jax.ShapeDtypeStruct((items, 4, part, width), HALF),
        ],
        compiler_params=params(),
        cost_estimate=cost(3.2e9, 12e6),
    )(images, order_matrix(), weight)


def spread_patches(tokens, weight, base, transposed, dtype):
    items, _, part, width = tokens.shape
    _, rows, columns, channels = base.shape
    steps = rows // 4

    def kernel(tokens, order, weight, base, result, product):
        values = dot(tokens[0].reshape(4 * part, width), weight[...], NT if transposed else NN)
        product[...] = values.astype(HALF).reshape(4, part, 4 * channels)

        def arrange(k, carry):
            at = pl.ds(pl.multiple_of(k * ROW, ROW), ROW)
            block = jnp.concatenate(
                [product[group, at, ab * channels : (ab + 1) * channels] for ab in range(4) for group in range(4)], axis=0
            )
            block = dot(order[...], block, TN).reshape(4, columns, channels)
            here = pl.ds(k * 4, 4)
            result[0, here] = (base[0, here].astype(F32) + block).astype(dtype)
            return carry

        lax.fori_loop(0, steps, arrange, 0)

    image = pl.BlockSpec((1, rows, columns, channels), lambda k: (k, 0, 0, 0))
    return pl.pallas_call(
        kernel,
        name="spread_patches",
        grid=(items,),
        in_specs=[
            pl.BlockSpec((1, 4, part, width), lambda k: (k, 0, 0, 0)),
            whole((16 * ROW, 16 * ROW)),
            whole(weight.shape),
            image,
        ],
        out_specs=image,
        out_shape=jax.ShapeDtypeStruct(base.shape, dtype),
        scratch_shapes=[pltpu.VMEM((4, part, 4 * channels), HALF)],
        compiler_params=params(),
        cost_estimate=cost(3.2e9, 12e6),
    )(tokens, order_matrix(), weight, base)


def modulation_forward(bucket, time_table, w_modulate):
    width = time_table.shape[1]
    columns = w_modulate.shape[1]
    block = columns // 6

    def kernel(bucket, table, weight, result):
        row = table[pl.ds(bucket[0] % 8, 1), :].astype(F32)
        row = (row * jax.nn.sigmoid(row)).astype(HALF)
        result[...] = dot(jnp.broadcast_to(row, (8, width)), weight[...], NN)

    return pl.pallas_call(
        kernel,
        name="modulation_forward",
        grid_spec=pltpu.PrefetchScalarGridSpec(
            num_scalar_prefetch=1,
            grid=(6,),
            in_specs=[
                pl.BlockSpec((8, width), lambda k, bucket: (bucket[0] // 8, 0)),
                pl.BlockSpec((width, block), lambda k, bucket: (0, k)),
            ],
            out_specs=pl.BlockSpec((8, block), lambda k, bucket: (0, k)),
        ),
        out_shape=jax.ShapeDtypeStruct((8, columns), F32),
        compiler_params=params(),
        cost_estimate=cost(1e9, 7e6),
    )(bucket, time_table.astype(F32), w_modulate)


def modulation_backward(every_grad, every_bucket, own_table, own_rows):
    items, columns = every_grad.shape
    entries, slice_width = own_table.shape

    def kernel(grads, buckets, table, rows, table_grad, weight_grad):
        at = lax.broadcasted_iota(jnp.int32, (entries, items), 0)
        chosen = jnp.where(at == buckets[...], 1.0, 0.0).astype(HALF)
        embedding = dot(chosen, table[...], TN)
        sigmoid = jax.nn.sigmoid(embedding)
        active = (embedding * sigmoid).astype(HALF)
        weight_grad[...] = dot(active, grads[...], TN)
        active_grad = dot(grads[...], rows[...], NT)
        grad = active_grad * sigmoid * (1.0 + embedding * (1.0 - sigmoid))
        first = grad.astype(HALF)
        second = (grad - first.astype(F32)).astype(HALF)
        table_grad[...] = dot(chosen, first, NN) + dot(chosen, second, NN)

    return pl.pallas_call(
        kernel,
        name="modulation_backward",
        out_shape=[
            jax.ShapeDtypeStruct((entries, slice_width), F32),
            jax.ShapeDtypeStruct((slice_width, columns), F32),
        ],
        compiler_params=params(),
        cost_estimate=cost(1e9, 4e6),
    )(every_grad, every_bucket, own_table, own_rows)


def own_columns(values, index, count):
    width = values.shape[1] // count
    return lax.dynamic_slice_in_dim(values, index * width, width, axis=1)


def bit_count(size):
    return size.bit_length() - 1


def swap(value, bit):
    name, place = bit
    size = lax.axis_size(name)
    return lax.ppermute(value, name, [(k, k ^ (1 << place)) for k in range(size)])


def own_bit(bit):
    name, place = bit
    return (lax.axis_index(name) >> place) & 1


def added(kept, received):
    return (kept.astype(F32) + received.astype(F32)).astype(HALF)


def pick(value, index, axis):
    return lax.dynamic_index_in_dim(value, index, axis=axis, keepdims=False)


def gather_bits(value, bits):
    for bit in bits:
        other = swap(value, bit)
        mine = own_bit(bit)
        value = jnp.stack([jnp.where(mine == 0, value, other), jnp.where(mine == 0, other, value)])
    return value


def mesh_bits():
    row_bits = [("row", bit) for bit in range(bit_count(lax.axis_size("row")))]
    dp_bits = [("dp", bit) for bit in range(bit_count(lax.axis_size("dp")))]
    return row_bits, dp_bits


def by_core(array, count, lanes):
    rows, columns = array.shape
    view = array.reshape(count, 2, rows // count // 2, columns // lanes, lanes)
    return view.transpose(0, 3, 1, 2, 4)


def joined_rows(sums, columns):
    return sums.transpose(0, 2, 1, 3).reshape(-1, columns)


class Halving:
    def __init__(self, arrays, order):
        row_bits, dp_bits = mesh_bits()
        self.dims, self.value = (None, None)
        self.arrays = arrays
        self.y_bits, self.dp_bits, self.core = (row_bits[1:], dp_bits, row_bits[0])
        named = {"y": self.y_bits, "a": dp_bits[:1], "b": dp_bits[1:2], "c": dp_bits[2:]}
        self.order = sum((named[letter] for letter in order), [])

    def step(self):
        if self.value is None:
            mine = own_bit(self.core)
            count = 1 << len(self.dp_bits)
            halves = []
            for index in (mine, 1 - mine):
                picked = [pick(v, index, 2).reshape(count, -1, v.shape[-1]) for v in self.arrays]
                halves.append(picked[0] if len(picked) == 1 else jnp.concatenate(picked, axis=1))
            value = added(halves[0], swap(halves[1], self.core))
            self.dims = self.dp_bits[::-1] + self.y_bits[::-1]
            rows = value.shape[1] >> len(self.y_bits)
            self.value = value.reshape((2,) * len(self.dims) + (rows, value.shape[2]))
            self.arrays = None
        elif self.order:
            bit = self.order.pop(0)
            at = self.dims.index(bit)
            mine = own_bit(bit)
            received = swap(pick(self.value, 1 - mine, at), bit)
            self.value = added(pick(self.value, mine, at), received)
            self.dims.pop(at)


class Doubling:
    def __init__(self, value, bits):
        self.value, self.order = (value, list(bits))

    def step(self):
        if self.order:
            self.value = gather_bits(self.value, [self.order.pop(0)])


def advance(parts, *others):
    for part in parts:
        part.step()
    flat = lax.optimization_barrier(tuple(part.value for part in parts) + others)
    for part, value in zip(parts, flat):
        part.value = value
    return flat[len(parts) :]


def body(
    latents,
    buckets,
    cotangent,
    time_table,
    w_modulate,
    conv_block,
    w_qkv,
    w_proj,
    w_fc1,
    conv_ffn,
    w_fc2,
    w_down,
    w_up,
):
    row_count = lax.axis_size("row")
    row_index = lax.axis_index("row")
    dp_count = lax.axis_size("dp")
    dp_index = lax.axis_index("dp")
    row_bits, dp_bits = mesh_bits()
    width = w_proj.shape[0]
    rows = width // dp_count
    taps_block = conv_block.astype(F32)
    taps_ffn = conv_ffn.astype(F32)

    def exchange(tokens):
        return lax.all_to_all(tokens, "row", split_axis=0, concat_axis=0, tiled=True)

    patches, sending = gather_patches(latents, w_down, False)
    arrived = exchange(sending)
    cot_patches, leaving_grad = gather_patches(cotangent, w_up, True)
    arrived_grad = exchange(leaving_grad)
    own_bucket = lax.dynamic_slice_in_dim(buckets, row_index, 1)
    pieces = modulation_forward(own_bucket, time_table, w_modulate)[0].reshape(6, width)
    every_bucket = gather_bits(buckets, dp_bits).reshape(1, -1)

    mixed_one, normed_one, merged, attended, mixed_two, normed_two = attention_forward(
        arrived, pieces, taps_block, w_qkv, w_proj
    )
    own_patches = exchange(lax.optimization_barrier((patches, arrived_grad))[0])

    hidden_width = conv_ffn.shape[1]
    fc1_grad, fc2_grad, ffn_taps, mixed_grad, leaving, vectors_two = ffn_both(
        arrived_grad, normed_two, mixed_two, pieces, w_fc1, taps_ffn, w_fc2, dp_count
    )
    split = is_split(width, hidden_width, dp_count)
    blocks = hidden_width // dp_count // 128 if split else 1
    if split:
        fc2_grad = fc2_grad.reshape(dp_count, blocks, 2, -1, 256)
    else:
        fc1_grad = by_core(fc1_grad, dp_count, 256)
        fc2_grad = by_core(fc2_grad, dp_count, 256).transpose(0, 2, 1, 3, 4)
        fc2_grad = fc2_grad.reshape(dp_count, 1, 2, -1, 256)
    mixed_grad, own_patches = lax.optimization_barrier((mixed_grad, own_patches))
    returned = exchange(leaving)
    first = Halving([fc1_grad], "yabc")
    second = Halving([fc2_grad], "abyc")
    one_grad, both_grad, vectors_one = attention_backward(
        mixed_grad, mixed_one, normed_one, merged, attended, pieces, w_qkv, w_proj, dp_count, split
    )
    if not split:
        both_grad = by_core(both_grad, dp_count, 384)
    modulation_grad = jnp.concatenate([vectors_one, vectors_two], axis=0).reshape(6 * width)
    one_grad, both_grad, modulation_grad, returned = advance(
        [first, second], one_grad, both_grad, modulation_grad.astype(HALF), returned
    )

    third = Halving([both_grad], "yabc")
    shared = Doubling(modulation_grad, row_bits + dp_bits)
    entering_back, block_taps = entry_backward(one_grad, arrived, taps_block)
    entering_grad = exchange(entering_back)
    down_grad = jnp.einsum(
        "agte,agtd->ed", own_patches, entering_back, preferred_element_type=F32
    ).astype(HALF)
    up_grad = jnp.einsum(
        "agtd,agte->de", returned, cot_patches, preferred_element_type=F32
    ).astype(HALF)
    output = spread_patches(returned, w_up, latents, False, HALF)
    down_grad, up_grad, block_taps, entering_grad, output = advance(
        [first, second, third, shared], down_grad, up_grad, block_taps, entering_grad, output
    )

    taps = jnp.concatenate(
        [ffn_taps.reshape(9, dp_count, -1), block_taps.reshape(9, dp_count, -1)], axis=2
    ).transpose(1, 0, 2)
    taps = jnp.pad(taps, ((0, 0), (0, 55), (0, width - taps.shape[2])))
    taps = taps.reshape(64 * dp_count, width).astype(HALF)
    fourth = Halving([by_core(up_grad, dp_count, w_up.shape[1])], "yabc")
    fifth = Halving([by_core(down_grad, dp_count, width), by_core(taps, dp_count, width)], "byac")
    parts = [first, second, third, fourth, fifth, shared]
    latents_grad = spread_patches(entering_grad, w_down, cotangent, True, F32)
    (latents_grad,) = advance(parts, latents_grad)
    while first.order or second.order:
        advance(parts)
    back_bits = row_bits[1:] + row_bits[:1]
    fc_sums = [Doubling(first.value, back_bits), Doubling(second.value, back_bits)]
    parts = [*fc_sums, third, fourth, fifth, shared]
    while shared.order:
        advance(parts)
    table_grad, modulate_grad = modulation_backward(
        shared.value.reshape(-1, 6 * width),
        every_bucket,
        own_columns(time_table, dp_index, dp_count),
        lax.dynamic_slice_in_dim(w_modulate, dp_index * rows, rows, axis=0),
    )
    parts = [*fc_sums, third, fourth, fifth]
    while fc_sums[0].order or third.order or fourth.order or fifth.order:
        advance(parts)
    rest = [Doubling(part.value, back_bits) for part in (third, fourth, fifth)]
    while rest[0].order:
        for part in rest:
            part.step()
    fc1_sums, fc2_sums, both_sums, up_sums, last_sums = [
        part.value.reshape(2, -1, part.value.shape[-1]).astype(F32) for part in [*fc_sums, *rest]
    ]
    fc1_final = joined_rows(fc1_sums.reshape(2, hidden_width // 256, -1, 256), hidden_width)
    fc2_final = fc2_sums.reshape(2, blocks, width // 256, -1, 256).transpose(1, 0, 3, 2, 4)
    both_final = joined_rows(both_sums.reshape(2, 8, -1, 384), 4 * width)
    up_final = up_sums.reshape(rows, w_up.shape[1])
    down_rows = w_down.shape[0] // dp_count
    down_final = last_sums[:, : down_rows // 2].reshape(down_rows, width)
    taps_final = last_sums[0, down_rows // 2 :]
    per_dp = hidden_width // dp_count
    return (
        output,
        latents_grad,
        table_grad,
        modulate_grad,
        taps_final[:9, per_dp : per_dp + rows],
        both_final[:, : 3 * width],
        both_final[:, 3 * width :],
        fc1_final,
        taps_final[:9, :per_dp],
        fc2_final.reshape(-1, width),
        down_final,
        up_final,
    )


def solution(mesh):
    in_specs = (
        P("dp", "row", None, None),
        P("dp"),
        P("dp", "row", None, None),
        P(),
        P(),
        P(),
        P(),
        P(),
        P(),
        P(),
        P(),
        P(),
        P(),
    )
    out_specs = (
        P("dp", "row", None, None),
        P("dp", "row", None, None),
        P(None, "dp"),
        P("dp", None),
        P(None, "dp"),
        P("dp", None),
        P("dp", None),
        P("dp", None),
        P(None, "dp"),
        P("dp", None),
        P("dp", None),
        P("dp", None),
    )
    return jax.shard_map(body, mesh=mesh, in_specs=in_specs, out_specs=out_specs, check_vma=False)
```
